512 devices in a mesh: frame: 16 (over y, z_lo), tile: 32 (over x, z_hi, core).
Axes of the slice: x: 4, y: 4, z: 16 (z_hi: 4, z_lo: 4; z = z_hi * 4 + z_lo), core: 2. Of those that a mesh axis runs over, the one named last changes fastest.
Arguments:
- latents: bfloat16 [16, 320, 8192], P('frame', None, 'tile'), may hold values from -80 to 80
- out_grad: bfloat16 [16, 320, 8192], P('frame', None, 'tile'), may hold values from -6 to 6
- w_spatial: bfloat16 [320, 2880], P('tile', 'frame'), may hold values from -0.109375 to 0.109375
- w_temporal: bfloat16 [320, 960], P('tile', 'frame'), may hold values from -0.1875 to 0.1875
- norm_gain: float32 [320], replicated, may hold values from 0.5 to 1.5
- norm_shift: float32 [320], replicated, may hold values from -1 to 1
- heights: int32 [32], P('tile'), may hold values from 8 to 16, as said below
Outputs:
- grad_input: bfloat16 [16, 320, 8192], P('frame', None, 'tile')
- grad_spatial: float32 [320, 2880], P('tile', 'frame')
- grad_temporal: float32 [320, 960], P('tile', 'frame')
- grad_gain: float32 [320], replicated
- grad_shift: float32 [320], replicated
The draws below stay inside these ranges and needn't reach their ends.
Inputs may be any that keep to these rules, and one draw needn't show every extreme that they name: `heights`: each entry is a multiple of 8; in every draw at least one strip has 16 live rows.
All inputs are finite; a program needn't handle non-finite values.
Results may differ from the reference program's by a relative error of at most 0.028.
Values may be sent and summed in bfloat16 or wider, within the bound.
No kernel may reach another device: no remote copies, remote signals or barrier semaphores. Data moves between devices by JAX's collectives and lax.ppermute only.
A program may use at most 64 MiB of HBM per device.

```python
import jax
import jax.numpy as jnp
from jax import lax

CHANNELS = 320
GROUPS = 32
COLUMNS = 16
STRIP_ROWS = 16
FRAMES = 16
STRIPS = 32
PIXELS = 8192


def draw_latents(key, part):
    key_base, key_scale, key_offset = jax.random.split(key, 3)
    frame_pos = jnp.arange(FRAMES, dtype=jnp.float32) / max(FRAMES - 1, 1)
    strip_pos = (jnp.arange(PIXELS, dtype=jnp.int32) // (STRIP_ROWS * COLUMNS)).astype(jnp.float32) / max(STRIPS - 1, 1)
    chan_scale = jnp.exp(jax.random.uniform(key_scale, (CHANNELS,), jnp.float32, jnp.log(0.4), jnp.log(4.0)))
    offset = jax.random.uniform(key_offset, (CHANNELS,), jnp.float32, -1.0, 1.0)
    base = jnp.clip(jax.random.normal(key_base, (FRAMES, CHANNELS, PIXELS), jnp.float32), -6.0, 6.0)
    rise = 1.0 + frame_pos[:, None, None] + strip_pos[None, None, :]
    values = offset[None, :, None] + chan_scale[None, :, None] * rise * base
    return values.astype(jnp.bfloat16)


def draw_heights(key, part):
    key_tall, key_pick = jax.random.split(key)
    tall_strip = jax.random.randint(key_tall, (STRIPS,), 0, 8) == 0
    chosen = jax.random.randint(key_pick, (), 0, STRIPS)
    tall_strip = tall_strip | (jnp.arange(STRIPS, dtype=jnp.int32) == chosen)
    return jnp.where(tall_strip, STRIP_ROWS, 8).astype(jnp.int32)


def raised(entries, key, source, target, shards_of, factor):
    def block_of(dim):
        return (jnp.arange(entries.shape[dim]) // (entries.shape[dim] // shards_of)).reshape((-1,) + (1,) * (entries.ndim - 1 - dim))

    first = jax.random.permutation(key, shards_of)[block_of(target)]
    second = (block_of(target) + shards_of // 2) % shards_of
    return jnp.where((block_of(source) == first) | (block_of(source) == second), factor * entries, entries)


def level_of(own_key, shape, cuts, smallest, high):
    factor_of = 1.0
    for dim, parts in cuts:
        steps = jax.random.uniform(jax.random.fold_in(jax.random.fold_in(own_key, 6), dim), (parts,), jnp.float32, smallest / len(cuts), high / len(cuts))
        factor_of = factor_of * jnp.repeat(jnp.exp(steps), shape[dim] // parts).reshape((-1,) + (1,) * (len(shape) - 1 - dim))
    return factor_of


def gaussian(key, extent, spread, limit, cuts=(), kind=jnp.bfloat16):
    gain = level_of(key, extent, cuts, -0.22, 0.18) if cuts else 1.0
    array = jax.random.normal(key, extent, jnp.float32) * spread * gain
    return jnp.minimum(jnp.maximum(array, -limit), limit).astype(kind)


def heavy_noise(key, dims, scale, bound, cuts, heavy, held_as=jnp.bfloat16):
    entries = scale * jax.random.normal(key, dims, jnp.float32)
    if cuts:
        entries = entries * level_of(key, dims, cuts, -0.22, 0.18)
    return jnp.clip(raised(entries, jax.random.fold_in(key, 3), *heavy), -bound, bound).astype(held_as)


def setup_inputs(seed: int = 0) -> dict:
    key_of = jax.random.split(jax.random.key(seed), 8)
    latents = draw_latents(jax.random.fold_in(key_of[7], 71), 0)
    out_grad = heavy_noise(key_of[1], (FRAMES, CHANNELS, PIXELS), 1.0, 6.0, ((0, 16), (2, 32)), (2, 1, 32, 2.75))
    w_spatial = gaussian(key_of[2], (CHANNELS, 9 * CHANNELS), (9 * CHANNELS) ** -0.5, 0.109375, ((0, 32), (1, 16)))
    w_temporal = gaussian(key_of[3], (CHANNELS, 3 * CHANNELS), (3 * CHANNELS) ** -0.5, 0.1875, ((0, 32), (1, 16)))
    norm_gain = jnp.clip(jax.random.uniform(key_of[4], (CHANNELS,), jnp.float32, 0.5, 1.5), 0.5, 1.5)
    norm_shift = jnp.clip(jax.random.uniform(key_of[5], (CHANNELS,), jnp.float32, -1.0, 1.0), -1.0, 1.0)
    heights = draw_heights(jax.random.fold_in(key_of[7], 71), 0)
    return {"latents": latents, "out_grad": out_grad, "w_spatial": w_spatial, "w_temporal": w_temporal, "norm_gain": norm_gain, "norm_shift": norm_shift, "heights": heights}


EPSILON = 1e-05

def neighbor_tables(heights):
    slot_index = jnp.arange(STRIPS * STRIP_ROWS, dtype=jnp.int32)
    strip_index = slot_index // STRIP_ROWS
    row_within = slot_index % STRIP_ROWS
    own_height = heights[strip_index]
    previous_height = heights[jnp.maximum(strip_index - 1, 0)]
    live_rows = row_within < own_height
    above_index = jnp.where(row_within > 0, slot_index - 1, (strip_index - 1) * STRIP_ROWS + previous_height - 1)
    above_valid = live_rows & ((row_within > 0) | (strip_index > 0))
    below_index = jnp.where(row_within + 1 < own_height, slot_index + 1, (strip_index + 1) * STRIP_ROWS)
    below_valid = live_rows & ((row_within + 1 < own_height) | (strip_index < STRIPS - 1))
    last_slot = STRIPS * STRIP_ROWS - 1
    return (live_rows, jnp.clip(above_index, 0, last_slot), above_valid, jnp.clip(below_index, 0, last_slot), below_valid)

def spatial_columns(field_grid, tables):
    live_rows, above_index, above_valid, below_index, below_valid = tables
    zero_value = jnp.zeros((), field_grid.dtype)
    upper_rows = jnp.where(above_valid[None, :, None], jnp.take(field_grid, above_index, axis=1), zero_value)
    lower_rows = jnp.where(below_valid[None, :, None], jnp.take(field_grid, below_index, axis=1), zero_value)
    pieces = []
    for rows_here in (upper_rows, field_grid, lower_rows):
        padded = jnp.pad(rows_here, ((0, 0), (0, 0), (1, 1)))
        for col_step in range(3):
            pieces.append(padded[:, :, col_step:col_step + COLUMNS])
    stacked = jnp.stack(pieces, axis=0)
    return stacked.reshape(9 * field_grid.shape[0], field_grid.shape[1] * COLUMNS)

def flip_taps(weight, tap_count):
    outputs = weight.shape[0]
    return jnp.transpose(weight.reshape(outputs, tap_count, -1)[:, ::-1, :], (2, 1, 0)).reshape(-1, tap_count * outputs)

def strip_partials(left_side, right_side):
    left_strips = left_side.astype(jnp.float32).reshape(left_side.shape[0], STRIPS, -1)
    right_strips = right_side.astype(jnp.float32).reshape(right_side.shape[0], STRIPS, -1)
    strip_parts = jnp.einsum('otp,ktp->tok', left_strips, right_strips, precision=lax.Precision.HIGHEST)
    rounded = lax.optimization_barrier(strip_parts.astype(jnp.bfloat16))
    return lax.optimization_barrier(jnp.sum(rounded.astype(jnp.float32), axis=0))

def reference(latents, out_grad, w_spatial, w_temporal, norm_gain, norm_shift, heights):
    tables = neighbor_tables(heights)
    live_cells = jnp.repeat(tables[0], COLUMNS)
    live_float = live_cells.astype(jnp.float32)
    group_size = CHANNELS // GROUPS
    rows_total = STRIPS * STRIP_ROWS
    latent_full = latents.astype(jnp.float32)
    masked = latent_full * live_float[None, None, :]
    chan_sum = lax.optimization_barrier(jnp.sum(masked, axis=(0, 2)))
    chan_square = lax.optimization_barrier(jnp.sum(masked * latent_full, axis=(0, 2)))
    position_count = FRAMES * jnp.sum(heights).astype(jnp.float32) * COLUMNS
    group_count = position_count * group_size
    group_mean = chan_sum.reshape(GROUPS, group_size).sum(1) / group_count
    group_var = chan_square.reshape(GROUPS, group_size).sum(1) / group_count - group_mean * group_mean
    group_rstd = lax.rsqrt(group_var + EPSILON)
    mean_column = jnp.repeat(group_mean, group_size)[:, None]
    rstd_column = jnp.repeat(group_rstd, group_size)[:, None]
    gain_column = norm_gain.astype(jnp.float32)[:, None]
    shift_column = norm_shift.astype(jnp.float32)[:, None]

    def frame_norm(frame_latent):
        normed = (frame_latent.astype(jnp.float32) - mean_column) * rstd_column
        pre_act = gain_column * normed + shift_column
        activated = jnp.where(live_cells[None, :], jax.nn.silu(pre_act), 0.0).astype(jnp.bfloat16)
        return (normed, pre_act, activated)

    def frame_forward(frame_latent):
        activated = frame_norm(frame_latent)[2]
        columns_here = spatial_columns(activated.reshape(CHANNELS, rows_total, COLUMNS), tables)
        spatial_raw = jnp.dot(w_spatial, columns_here, preferred_element_type=jnp.float32)
        return jnp.where(live_cells[None, :], spatial_raw, 0.0).astype(jnp.bfloat16)
    spatial_out = lax.map(frame_forward, latents)
    grad_masked = jnp.where(live_cells[None, None, :], out_grad, jnp.zeros((), jnp.bfloat16))
    zero_frame = jnp.zeros((1, CHANNELS, PIXELS), jnp.bfloat16)
    spatial_pad = jnp.concatenate([zero_frame, spatial_out, zero_frame], axis=0)
    grad_pad = jnp.concatenate([zero_frame, grad_masked, zero_frame], axis=0)
    temporal_flip = flip_taps(w_temporal, 3)
    spatial_flip = flip_taps(w_spatial, 9)

    def frame_backward(running, frame_index):
        sum_spatial, sum_temporal, sum_gain, sum_shift = running
        frame_latent = lax.dynamic_index_in_dim(latents, frame_index, 0, keepdims=False)
        normed, pre_act, activated = frame_norm(frame_latent)
        act_columns = spatial_columns(activated.reshape(CHANNELS, rows_total, COLUMNS), tables)
        grad_frame = lax.dynamic_index_in_dim(grad_masked, frame_index, 0, keepdims=False)
        spat_window = lax.dynamic_slice_in_dim(spatial_pad, frame_index, 3, 0).reshape(3 * CHANNELS, PIXELS)
        grad_window = lax.dynamic_slice_in_dim(grad_pad, frame_index, 3, 0).reshape(3 * CHANNELS, PIXELS)
        grad_spat = jnp.dot(temporal_flip, grad_window, preferred_element_type=jnp.float32)
        grad_spat = jnp.where(live_cells[None, :], grad_spat, 0.0).astype(jnp.bfloat16)
        grad_columns = spatial_columns(grad_spat.reshape(CHANNELS, rows_total, COLUMNS), tables)
        grad_act = jnp.dot(spatial_flip, grad_columns, preferred_element_type=jnp.float32)
        sigmoid_act = jax.nn.sigmoid(pre_act)
        grad_pre = jnp.where(live_cells[None, :], grad_act * sigmoid_act * (1.0 + pre_act * (1.0 - sigmoid_act)), 0.0)
        sum_temporal = sum_temporal + strip_partials(grad_frame, spat_window)
        sum_spatial = sum_spatial + strip_partials(grad_spat, act_columns)
        sum_gain = sum_gain + lax.optimization_barrier(jnp.sum(grad_pre * normed, axis=1))
        sum_shift = sum_shift + lax.optimization_barrier(jnp.sum(grad_pre, axis=1))
        return ((sum_spatial, sum_temporal, sum_gain, sum_shift), grad_pre)
    start = (jnp.zeros((CHANNELS, 9 * CHANNELS), jnp.float32), jnp.zeros((CHANNELS, 3 * CHANNELS), jnp.float32), jnp.zeros((CHANNELS,), jnp.float32), jnp.zeros((CHANNELS,), jnp.float32))
    finals, grad_pre_all = lax.scan(frame_backward, start, jnp.arange(FRAMES, dtype=jnp.int32))
    sum_spatial, sum_temporal, chan_gain, chan_shift = finals
    shift_sum = (norm_gain * chan_shift).reshape(GROUPS, group_size).sum(1) / group_count
    gain_sum = (norm_gain * chan_gain).reshape(GROUPS, group_size).sum(1) / group_count
    shift_column_sum = jnp.repeat(shift_sum, group_size)[:, None]
    gain_column_sum = jnp.repeat(gain_sum, group_size)[:, None]

    def frame_input(pair):
        frame_latent, grad_pre, grad_frame = pair
        normed = (frame_latent.astype(jnp.float32) - mean_column) * rstd_column
        result = grad_frame.astype(jnp.float32) + rstd_column * (gain_column * grad_pre - shift_column_sum - normed * gain_column_sum)
        return jnp.where(live_cells[None, :], result, 0.0).astype(jnp.bfloat16)
    grad_input = lax.map(frame_input, (latents, grad_pre_all, grad_masked))
    grad_scale = lax.rsqrt(position_count)
    return (grad_input, grad_scale * sum_spatial, grad_scale * sum_temporal, grad_scale * chan_gain, grad_scale * chan_shift)
```

```python
import functools

import jax
import jax.numpy as jnp
from jax import lax
from jax.experimental import pallas as pl
from jax.experimental.pallas import tpu as pltpu
from jax.sharding import Mesh
from jax.sharding import PartitionSpec as P

GROUPS = 32
GROUP_SIZE = 10
CHANNELS = 320
COLUMNS = 16
STRIPS = 32
FRAMES = 16
CELLS = 256
EXT = 384
BELOW = 256
ABOVE = 368
SPAN = 720
SPAN_T = 240
WIDE = 768
PACK = 1024
EPSILON = 1e-05

TILE = ("tile_0", "tile_1", "tile_2")
FRAME = ("frame_0", "frame_1")
ROW_Z = ("frame_1", "tile_1")
PLANE = ("frame_0", "tile_0")
PLANE_CORE = ("frame_0", "tile_0", "tile_2")

bf16 = jnp.bfloat16
f32 = jnp.float32
NT = (((1,), (1,)), ((), ()))


def iota(shape, dim):
    return lax.broadcasted_iota(jnp.int32, shape, dim)


def dot(a, b):
    return jnp.dot(a, b, preferred_element_type=f32)


def dot_nt(a, b):
    return lax.dot_general(a, b, NT, preferred_element_type=f32)


def zero_one(mask):
    return jnp.where(mask, 1.0, 0.0).astype(bf16)


def to_all(value, axes):
    peers = lax.axis_size(axes)
    copies = jnp.broadcast_to(value[None], (peers, *value.shape))
    return lax.all_to_all(copies, axes, 0, 0, tiled=True)


def column_place(z_low):
    source = iota((256, PACK), 0)
    place = iota((256, PACK), 1)
    spatial = (source < 180) & (place == source + z_low * 180)
    temporal = (source >= 180) & (source < 240)
    temporal &= place == source + (WIDE - 180 + z_low * 60)
    return zero_one(spatial | temporal)


def row_place(shape, dim_small, dim_padded):
    small = iota(shape, dim_small)
    padded = iota(shape, dim_padded)
    match = small < 0
    for a in range(4):
        match |= (small >= 10 * a) & (small < 10 * a + 10) & (padded == small + 6 * a)
    return zero_one(match)


def pack_kernel(blocks, out):
    total = jnp.zeros((64, PACK), f32)
    for z_low in range(4):
        total += dot(blocks[z_low], column_place(z_low))
    out[...] = dot(row_place((40, 64), 0, 1), total.astype(bf16)).astype(bf16)


def unpack_kernel(terms, out):
    total = terms[0].astype(f32)
    for n in range(1, 16):
        total += terms[n].astype(f32)
    rows = dot(row_place((64, 40), 1, 0), total.astype(bf16)).astype(bf16)
    for z_low in range(4):
        out[z_low] = dot_nt(rows, column_place(z_low)).astype(bf16)


def stat_columns(stats, group):
    total = jnp.sum(stats[...], axis=0, keepdims=True)
    lane = iota((CHANNELS, 128), 1)

    def pick(mask):
        return jnp.sum(jnp.where(mask, total, 0.0), axis=1, keepdims=True)

    positions = pick(lane == 2 * GROUPS)
    count = positions * GROUP_SIZE
    mean = pick(lane == group) / count
    rstd = lax.rsqrt(pick(lane == group + GROUPS) / count - mean * mean + EPSILON)
    return positions, count, mean, rstd


def turned(row):
    eye = iota((CHANNELS, CHANNELS), 0) == iota((CHANNELS, CHANNELS), 1)
    return jnp.sum(jnp.where(eye, row, 0.0), axis=1, keepdims=True)


def turned_back(column):
    eye = iota((CHANNELS, CHANNELS), 0) == iota((CHANNELS, CHANNELS), 1)
    return jnp.sum(jnp.where(eye, column, 0.0), axis=0, keepdims=True)


def pieces_of(start, stop, span):
    while start < stop:
        end = min(stop, (start // span + 1) * span)
        yield start // span, start % span, start, end - start
        start = end


def main_kernel(
    place, stats, gain, shift, order, order_row, group, latent, g_next, g_here, g_last,
    w_own, w_other, grad_own, grad_other, pre_grad, sums, cols, turned_s, turned_t, frames, taps,
):
    height = place[0]
    strip = place[1]
    lane = iota((1, EXT), 1)
    live = ((lane < CELLS) & ((lane >> 4) < height)) | (
        (lane >= BELOW) & (lane < BELOW + COLUMNS) & (strip < STRIPS - 1)
    ) | ((lane >= ABOVE) & (strip > 0))
    to_packed = zero_one(order[...] == iota((CHANNELS, CHANNELS), 1))
    to_plain = zero_one(iota((CHANNELS, CHANNELS), 0) == order_row[...])

    for y in range(4):
        whole = jnp.concatenate([w_own[y], w_other[y]], axis=0)
        across = whole.T
        turned_s[y * SPAN : (y + 1) * SPAN, :] = across[:SPAN]
        turned_t[y * SPAN_T : (y + 1) * SPAN_T, :] = across[WIDE : WIDE + SPAN_T]

    _, _, mean, rstd = stat_columns(stats, group[...])
    gain_column = turned(gain[...])
    shift_column = turned(shift[...])
    normed = (latent[...].astype(f32) - mean) * rstd
    pre_act = gain_column * normed + shift_column
    sigmoid = 1.0 / (1.0 + jnp.exp(-pre_act))
    active = jnp.where(live, pre_act * sigmoid, 0.0).astype(bf16)

    grad_spat = jnp.zeros((CHANNELS, EXT), f32)
    for k, ref in enumerate((g_next, g_here, g_last)):
        packed = dot(to_packed, ref[...]).astype(bf16)
        taps[:, k * CELLS : (k + 1) * CELLS] = packed[:, :CELLS]
        grad_spat += dot(turned_t[k * CHANNELS : (k + 1) * CHANNELS, :], packed)
    grad_spat = jnp.where(live, grad_spat, 0.0).astype(bf16)
    spat_packed = dot(to_packed, grad_spat).astype(bf16)

    for y in range(4):
        cols[y, SPAN:, :] = jnp.zeros((WIDE - SPAN, CELLS), bf16)
    cell = iota((1, CELLS), 1)
    source = iota((EXT, CELLS), 0)
    grad_act = jnp.zeros((CHANNELS, CELLS), f32)
    for k in range(9):
        row = (cell >> 4) + (k // 3 - 1)
        column = (cell & 15) + (k % 3 - 1)
        base = jnp.where(row < 0, ABOVE, jnp.where(row == height, BELOW, row * COLUMNS))
        wanted = jnp.where((column >= 0) & (column < COLUMNS), base + column, -1)
        move = zero_one(source == wanted)
        moved = dot(active, move).astype(bf16)
        for y, at, start, size in pieces_of(k * CHANNELS, (k + 1) * CHANNELS, SPAN):
            first = start - k * CHANNELS
            cols[y, at : at + size, :] = moved[first : first + size]
        back = 8 - k
        grad_act += dot(
            turned_s[back * CHANNELS : (back + 1) * CHANNELS, :],
            dot(spat_packed, move).astype(bf16),
        )

    spatial = jnp.zeros((CHANNELS, CELLS), f32)
    left = spat_packed[:, :CELLS]
    for y in range(4):
        whole = jnp.concatenate([w_own[y, :, :WIDE], w_other[y, :, :WIDE]], axis=0)
        spatial += dot(whole, cols[y])
        part = dot_nt(left, cols[y]).astype(bf16)
        grad_own[y, :, :WIDE] = part[:160]
        grad_other[y, :, :WIDE] = part[160:]
    own_live = live[:, :CELLS]
    spatial = jnp.where(own_live, spatial, 0.0).astype(bf16)
    spatial = dot(to_plain, spatial).astype(bf16)

    frames[...] = jnp.zeros(frames.shape, bf16)
    for k in range(3):
        for y, at, start, size in pieces_of(k * CHANNELS, (k + 1) * CHANNELS, SPAN_T):
            first = start - k * CHANNELS
            frames[y, at : at + size, k * CELLS : (k + 1) * CELLS] = spatial[first : first + size]
    for y in range(4):
        part = dot_nt(taps[...], frames[y]).astype(bf16)
        grad_own[y, :, WIDE:] = part[:160]
        grad_other[y, :, WIDE:] = part[160:]

    act = pre_act[:, :CELLS]
    sig = sigmoid[:, :CELLS]
    grad_pre = jnp.where(own_live, grad_act * sig * (1.0 + act * (1.0 - sig)), 0.0)
    pre_grad[...] = grad_pre
    chan_gain = jnp.sum(grad_pre * normed[:, :CELLS], axis=1, keepdims=True)
    chan_shift = jnp.sum(grad_pre, axis=1, keepdims=True)
    sums[...] = jnp.zeros(sums.shape, f32)
    sums[:, :CHANNELS] = turned_back(chan_gain)
    sums[:, EXT : EXT + CHANNELS] = turned_back(chan_shift)


def input_kernel(
    place, stats, gain, group, group_row, latent, g_here, pre_grad, sums, result, totals
):
    height = place[0]
    own_live = (iota((1, CELLS), 1) >> 4) < height
    positions, count, mean, rstd = stat_columns(stats, group[...])
    total = jnp.sum(sums[...], axis=0, keepdims=True)
    scale = lax.rsqrt(positions[:1, :1])
    totals[...] = total * scale
    same = group[...] == group_row[...]

    def over_group(row):
        return jnp.sum(jnp.where(same, gain[...] * row, 0.0), axis=1, keepdims=True) / count

    gain_sum = over_group(total[:, :CHANNELS])
    shift_sum = over_group(total[:, EXT : EXT + CHANNELS])
    normed = (latent[:, :CELLS].astype(f32) - mean) * rstd
    value = g_here[:, :CELLS].astype(f32) + rstd * (
        turned(gain[...]) * pre_grad[...] - shift_sum - normed * gain_sum
    )
    result[...] = jnp.where(own_live, value, 0.0).astype(bf16)


def call(kernel, outs, smem=0, scratch=(), inputs=1, flops=0, moved=0):
    vmem = pl.BlockSpec(memory_space=pltpu.VMEM)
    specs = [pl.BlockSpec(memory_space=pltpu.SMEM)] * smem + [vmem] * (inputs - smem)
    many = isinstance(outs, tuple)
    return pl.pallas_call(
        kernel,
        out_shape=outs,
        in_specs=specs,
        out_specs=tuple(vmem for _ in outs) if many else vmem,
        scratch_shapes=list(scratch),
        compiler_params=pltpu.CompilerParams(vmem_limit_bytes=48 << 20),
        cost_estimate=pl.CostEstimate(flops=flops, bytes_accessed=moved, transcendentals=0),
    )


def shape(dims, kind):
    return jax.ShapeDtypeStruct(dims, kind)


def step_by(value, axes, by):
    peers = lax.axis_size(axes)
    pairs = [(i, i + by) for i in range(peers) if 0 <= i + by < peers]
    return lax.ppermute(value, axes, pairs)


def swap_cores(value):
    return lax.ppermute(value, "tile_2", [(0, 1), (1, 0)])


def extended(own, above, below):
    gap = jnp.zeros((CHANNELS, ABOVE - BELOW - COLUMNS), own.dtype)
    return jnp.concatenate([own, below, gap, above], axis=1)


def local(latents, out_grad, w_spatial, w_temporal, norm_gain, norm_shift, heights):
    height = heights[0]
    core = lax.axis_index("tile_2")
    strip = lax.axis_index(TILE)
    place = jnp.stack([height, strip]).astype(jnp.int32)
    live = (jnp.arange(CELLS, dtype=jnp.int32) // COLUMNS < height)[None, :]
    latent = latents[0]
    grad = jnp.where(live, out_grad[0], jnp.zeros((), bf16))

    shard = jnp.concatenate([w_spatial, w_temporal], axis=1)
    shard = jnp.pad(shard, ((0, 6), (0, 16)))
    near = to_all(shard, ROW_Z).reshape(4, 64, 256)
    packed = call(pack_kernel, shape((40, PACK), bf16), flops=1 << 27, moved=1 << 18)(near)
    w_own = to_all(packed, PLANE).reshape(4, 160, PACK)
    w_other = swap_cores(w_own)

    wide = jnp.where(live, latent, jnp.zeros((), bf16)).astype(f32)
    chan_sum = jnp.sum(wide, axis=1)
    chan_square = jnp.sum(wide * wide, axis=1)
    own_stats = jnp.concatenate(
        [
            chan_sum.reshape(GROUPS, GROUP_SIZE).sum(1),
            chan_square.reshape(GROUPS, GROUP_SIZE).sum(1),
            (height * COLUMNS).astype(f32)[None],
            jnp.zeros((63,), f32),
        ]
    )[None]
    stats = jnp.sum(to_all(own_stats, ROW_Z), axis=0)
    stats = to_all(stats, PLANE_CORE)[:, 0]

    both = jnp.stack([latent, grad])
    tall = height == 16
    last = jnp.where(tall, both[:, :, 240:256], both[:, :, 112:128])
    above = step_by(last, TILE, 1)
    below = step_by(both[:, :, :COLUMNS], TILE, -1)
    latent_ext = extended(latent, above[0], below[0])
    grad_ext = extended(grad, above[1], below[1])
    grad_last = step_by(grad_ext, FRAME, 1)
    grad_next = step_by(grad_ext, FRAME, -1)

    packed_row = jnp.arange(CHANNELS, dtype=jnp.int32)
    half, rest = packed_row // 160, packed_row % 160
    order = rest // 40 * 80 + rest % 40 // 10 * 20 + rest % 10
    order = order + jnp.where(half == 0, core, 1 - core) * 10
    group = jnp.arange(CHANNELS, dtype=jnp.int32) // GROUP_SIZE
    gain_row, shift_row = norm_gain[None], norm_shift[None]
    block = shape((4, 160, PACK), bf16)
    grad_own, grad_other, pre_grad, sums = call(
        main_kernel,
        (block, block, shape((CHANNELS, CELLS), f32), shape((1, 2 * EXT), f32)),
        smem=1,
        inputs=13,
        scratch=(
            pltpu.VMEM((4, WIDE, CELLS), bf16),
            pltpu.VMEM((4 * SPAN, CHANNELS), bf16),
            pltpu.VMEM((4 * SPAN_T, CHANNELS), bf16),
            pltpu.VMEM((4, CELLS, 3 * CELLS), bf16),
            pltpu.VMEM((CHANNELS, 3 * CELLS), bf16),
        ),
        flops=5 << 30,
        moved=8 << 20,
    )(
        place, stats, gain_row, shift_row, order[:, None], order[None, :], group[:, None],
        latent_ext, grad_next, grad_ext, grad_last, w_own, w_other,
    )

    chan = jnp.sum(to_all(sums, ROW_Z), axis=0)
    chan = to_all(chan, PLANE_CORE)[:, 0]
    grad_input, totals = call(
        input_kernel,
        (shape((CHANNELS, CELLS), bf16), shape((1, 2 * EXT), f32)),
        smem=1,
        inputs=9,
        flops=1 << 22,
        moved=1 << 20,
    )(
        place, stats, gain_row, group[:, None], group[None, :], latent_ext, grad_ext,
        pre_grad, chan,
    )

    pair = grad_own.astype(f32) + swap_cores(grad_other).astype(f32)
    terms = lax.all_to_all(
        pair.astype(bf16).reshape(16, 40, PACK), PLANE, 0, 0, tiled=True
    )
    parts = call(unpack_kernel, shape((4, 64, 256), bf16), flops=1 << 27, moved=1 << 21)(terms)
    mine = lax.all_to_all(parts.reshape(16, 16, 256), ROW_Z, 0, 0, tiled=True)
    scale = lax.rsqrt(jnp.sum(stats[:, 2 * GROUPS]))
    mine = jnp.sum(mine.astype(f32), axis=0) * scale
    return (
        grad_input[None],
        mine[:10, :180],
        mine[:10, 180:240],
        totals[0, :CHANNELS],
        totals[0, EXT : EXT + CHANNELS],
    )


def solution(mesh):
    split = Mesh(
        mesh.devices.reshape(4, 4, 4, 4, 2), ("frame_0", "frame_1", "tile_0", "tile_1", "tile_2")
    )
    placed = (
        P(FRAME, None, TILE),
        P(FRAME, None, TILE),
        P(TILE, FRAME),
        P(TILE, FRAME),
        P(),
        P(),
        P(TILE),
    )
    return jax.shard_map(
        local,
        mesh=split,
        in_specs=placed,
        out_specs=(P(FRAME, None, TILE), P(TILE, FRAME), P(TILE, FRAME), P(), P()),
        check_vma=False,
    )
```

```python
import functools

import jax
import jax.numpy as jnp
from jax import lax
from jax.experimental import pallas as pl
from jax.experimental.pallas import tpu as pltpu
from jax.sharding import Mesh
from jax.sharding import PartitionSpec as P

GROUPS = 32
GROUP_SIZE = 10
CHANNELS = 320
COLUMNS = 16
STRIPS = 32
FRAMES = 16
CELLS = 256
EXT = 384
BELOW = 256
ABOVE = 368
SPAN = 720
SPAN_T = 240
WIDE = 768
PACK = 1024
EPSILON = 1e-05
SPARE = 10
TILE_AT = 640
FREE = 80

TILE = ("tile_0", "tile_1", "tile_2")
FRAME = ("frame_0", "frame_1")
ROW_Z = ("frame_1", "tile_1")
PLANE = ("frame_0", "tile_0")
PLANE_CORE = ("frame_0", "tile_0", "tile_2")

bf16 = jnp.bfloat16
f32 = jnp.float32
NT = (((1,), (1,)), ((), ()))


def iota(shape, dim):
    return lax.broadcasted_iota(jnp.int32, shape, dim)


def dot(a, b):
    return jnp.dot(a, b, preferred_element_type=f32)


def dot_nt(a, b):
    return lax.dot_general(a, b, NT, preferred_element_type=f32)


def zero_one(mask):
    return jnp.where(mask, 1.0, 0.0).astype(bf16)


def exchange(blocks, axes):
    return lax.all_to_all(blocks, axes, 0, 0, tiled=True)


def column_place(z_low):
    source = iota((256, PACK), 0)
    place = iota((256, PACK), 1)
    spatial = (source < 180) & (place == source + z_low * 180)
    temporal = (source >= 180) & (source < 240)
    temporal &= place == source + (WIDE - 180 + z_low * 60)
    return zero_one(spatial | temporal)


def row_place(shape, dim_small, dim_padded):
    small = iota(shape, dim_small)
    padded = iota(shape, dim_padded)
    match = small < 0
    for a in range(4):
        match |= (small >= 10 * a) & (small < 10 * a + 10) & (padded == small + 6 * a)
    return zero_one(match)


def rounded(value):
    return value.astype(bf16).astype(f32)


def pieces_in(value):
    first = rounded(value)
    second = rounded(value - first)
    return first, second, rounded(value - first - second)


def with_tile(block, tile):
    return jnp.concatenate([block[:, :TILE_AT], tile, block[:, WIDE:]], axis=1)


def start_kernel(place, latent, group, shard, out):
    height = place[0]
    live = (iota((1, CELLS), 1) >> 4) < height
    value = jnp.where(live, latent[...].astype(f32), 0.0)
    chan_sum = jnp.sum(value, axis=1, keepdims=True)
    chan_square = jnp.sum(value * value, axis=1, keepdims=True)
    lane = iota((CHANNELS, 128), 1)
    terms = jnp.where(lane == group[...], chan_sum, 0.0)
    terms += jnp.where(lane == group[...] + GROUPS, chan_square, 0.0)
    cells = (height * COLUMNS).astype(f32)
    stats = jnp.sum(terms, axis=0, keepdims=True)
    stats += jnp.where(iota((1, 128), 1) == 2 * GROUPS, cells, 0.0)
    row = iota((16, 128), 0)
    extra = jnp.zeros((16, 128), f32)
    for n, piece in enumerate(pieces_in(stats)):
        extra += jnp.where(row == SPARE + n, piece, 0.0)
    extra = jnp.concatenate([extra, jnp.zeros((16, 128), f32)], axis=1)
    block = (shard[...].astype(f32) + extra).astype(bf16)
    for n in range(16):
        out[n] = block


def pack_kernel(blocks, out):
    total = jnp.zeros((64, PACK), f32)
    stats = jnp.zeros((64, 128), f32)
    for z_low in range(4):
        total += dot(blocks[z_low], column_place(z_low))
        stats += blocks[z_low, :, :128].astype(f32)
    packed = dot(row_place((40, 64), 0, 1), total.astype(bf16))
    row = iota((64, 128), 0) & 15
    stats = jnp.where((row >= SPARE) & (row < SPARE + 3), stats, 0.0)
    stats = jnp.sum(stats, axis=0, keepdims=True)
    line = iota((40, 128), 0)
    lane = iota((40, 128), 1)
    wanted = (line, line + GROUPS, 0 * line + 2 * GROUPS)
    tile = packed[:, TILE_AT:WIDE]
    for q in range(3):
        mask = (lane == wanted[q]) & ((line < GROUPS) | (q == 2))
        column = jnp.sum(jnp.where(mask, stats, 0.0), axis=1, keepdims=True)
        for n, piece in enumerate(pieces_in(column)):
            tile += jnp.where(lane == FREE + 3 * q + n, piece, 0.0)
    packed = with_tile(packed, tile).astype(bf16)
    for n in range(16):
        out[n] = packed


def stat_columns(w_own, w_other, group):
    halves = []
    for ref in (w_own, w_other):
        half = jnp.zeros((40, 128), f32)
        for y in range(4):
            tile = ref[y, :, TILE_AT:WIDE].astype(f32).reshape(4, 40, 128)
            half += tile[0] + tile[1] + tile[2] + tile[3]
        halves.append(half)
    total = halves[0] + halves[1]
    line = iota((40, 128), 0)
    lane = iota((40, 128), 1)

    def quantity(q):
        mask = (lane >= FREE + 3 * q) & (lane < FREE + 3 * q + 3)
        return jnp.sum(jnp.where(mask, total, 0.0), axis=1, keepdims=True)

    def pick(q):
        across = jnp.sum(jnp.where(line == lane, quantity(q), 0.0), axis=0, keepdims=True)
        wide = iota((CHANNELS, 128), 1)
        return jnp.sum(jnp.where(wide == group, across, 0.0), axis=1, keepdims=True)

    positions = quantity(2)[:1]
    count = positions * GROUP_SIZE
    mean = pick(0) / count
    rstd = lax.rsqrt(pick(1) / count - mean * mean + EPSILON)
    return positions, mean, rstd


def sums_split(value):
    first = rounded(value)
    return first + pltpu.roll(rounded(value - first), 16, 1)


def sums_joined(tile):
    lane = iota((40, 128), 1)
    mask = (lane >= FREE) & (lane < FREE + 16)
    return jnp.where(mask, tile + pltpu.roll(tile, 112, 1), 0.0)


def pair_kernel(own, other, out):
    lane = iota((40, 128), 1)

    def body(n, _):
        total = own[n].astype(f32) + other[n].astype(f32)
        tile = total[:, TILE_AT:WIDE]
        tile = jnp.where(lane < FREE, tile, sums_split(sums_joined(tile)))
        out[n] = with_tile(total, tile).astype(bf16)
        return 0

    lax.fori_loop(0, 16, body, 0)


def unpack_kernel(terms, out):
    total = terms[0].astype(f32)
    for n in range(1, 16):
        total += terms[n].astype(f32)
    sums = pltpu.roll(sums_joined(total[:, TILE_AT:WIDE]), 128 - FREE, 1)
    for step in (16, 32, 64):
        sums += pltpu.roll(sums, step, 1)
    mine = (iota((40, 128), 1) >> 4) == (iota((40, 128), 0) & 7)
    sums = jnp.sum(jnp.where(mine, sums, 0.0).reshape(5, 8, 128), axis=1)
    first = rounded(sums)
    sums = jnp.concatenate([first, rounded(sums - first)], axis=1)
    row = iota((16, 256), 0)
    extra = jnp.zeros((16, 256), f32)
    for n in range(5):
        extra += jnp.where(row == SPARE + n, sums[n : n + 1], 0.0)
    extra = jnp.concatenate([extra] * 4, axis=0)
    rows = dot(row_place((64, 40), 1, 0), total.astype(bf16)).astype(bf16)
    for z_low in range(4):
        out[z_low] = (dot_nt(rows, column_place(z_low)) + extra).astype(bf16)


def turned(row):
    eye = iota((CHANNELS, CHANNELS), 0) == iota((CHANNELS, CHANNELS), 1)
    return jnp.sum(jnp.where(eye, row, 0.0), axis=1, keepdims=True)


def turned_back(column):
    eye = iota((CHANNELS, CHANNELS), 0) == iota((CHANNELS, CHANNELS), 1)
    return jnp.sum(jnp.where(eye, column, 0.0), axis=0, keepdims=True)


def pieces_of(start, stop, span):
    while start < stop:
        end = min(stop, (start // span + 1) * span)
        yield start // span, start % span, start, end - start
        start = end


def main_kernel(
    place, gain, shift, order, order_row, group, latent, g_next, g_here, g_last,
    w_own, w_other, grad_own, grad_other, pre_grad, norm, cols, turned_s, turned_t, frames, taps,
):
    height = place[0]
    strip = place[1]
    lane = iota((1, EXT), 1)
    live = ((lane < CELLS) & ((lane >> 4) < height)) | (
        (lane >= BELOW) & (lane < BELOW + COLUMNS) & (strip < STRIPS - 1)
    ) | ((lane >= ABOVE) & (strip > 0))
    to_packed = zero_one(order[...] == iota((CHANNELS, CHANNELS), 1))
    to_plain = zero_one(iota((CHANNELS, CHANNELS), 0) == order_row[...])

    for y in range(4):
        whole = jnp.concatenate([w_own[y], w_other[y]], axis=0)
        across = whole.T
        turned_s[y * SPAN : (y + 1) * SPAN, :] = across[:SPAN]
        turned_t[y * SPAN_T : (y + 1) * SPAN_T, :] = across[WIDE : WIDE + SPAN_T]

    positions, mean, rstd = stat_columns(w_own, w_other, group[...])
    lane_n = iota((CHANNELS, 128), 1)
    norm[...] = jnp.where(lane_n == 0, mean, jnp.where(lane_n == 1, rstd, positions))
    gain_column = turned(gain[...])
    shift_column = turned(shift[...])
    normed = (latent[...].astype(f32) - mean) * rstd
    pre_act = gain_column * normed + shift_column
    sigmoid = 1.0 / (1.0 + jnp.exp(-pre_act))
    active = jnp.where(live, pre_act * sigmoid, 0.0).astype(bf16)

    grad_spat = jnp.zeros((CHANNELS, EXT), f32)
    for k, ref in enumerate((g_next, g_here, g_last)):
        packed = dot(to_packed, ref[...]).astype(bf16)
        taps[:, k * CELLS : (k + 1) * CELLS] = packed[:, :CELLS]
        grad_spat += dot(turned_t[k * CHANNELS : (k + 1) * CHANNELS, :], packed)
    grad_spat = jnp.where(live, grad_spat, 0.0).astype(bf16)
    spat_packed = dot(to_packed, grad_spat).astype(bf16)

    for y in range(4):
        cols[y, SPAN:, :] = jnp.zeros((WIDE - SPAN, CELLS), bf16)
    cell = iota((1, CELLS), 1)
    source = iota((EXT, CELLS), 0)
    grad_act = jnp.zeros((CHANNELS, CELLS), f32)
    for k in range(9):
        row = (cell >> 4) + (k // 3 - 1)
        column = (cell & 15) + (k % 3 - 1)
        base = jnp.where(row < 0, ABOVE, jnp.where(row == height, BELOW, row * COLUMNS))
        wanted = jnp.where((column >= 0) & (column < COLUMNS), base + column, -1)
        move = zero_one(source == wanted)
        moved = dot(active, move).astype(bf16)
        for y, at, start, size in pieces_of(k * CHANNELS, (k + 1) * CHANNELS, SPAN):
            first = start - k * CHANNELS
            cols[y, at : at + size, :] = moved[first : first + size]
        back = 8 - k
        grad_act += dot(
            turned_s[back * CHANNELS : (back + 1) * CHANNELS, :],
            dot(spat_packed, move).astype(bf16),
        )

    own_live = live[:, :CELLS]
    act = pre_act[:, :CELLS]
    sig = sigmoid[:, :CELLS]
    grad_pre = jnp.where(own_live, grad_act * sig * (1.0 + act * (1.0 - sig)), 0.0)
    pre_grad[...] = grad_pre
    chan_gain = jnp.sum(grad_pre * normed[:, :CELLS], axis=1, keepdims=True)
    chan_shift = jnp.sum(grad_pre, axis=1, keepdims=True)
    spot = (iota((CHANNELS, 128), 0) & 7) + FREE
    sums = jnp.where(lane_n == spot, chan_gain, 0.0)
    sums += jnp.where(lane_n == spot + 8, chan_shift, 0.0)
    sums = sums_split(jnp.sum(sums.reshape(40, 8, 128), axis=1))
    sums = jnp.concatenate([sums] * 4, axis=0)

    spatial = jnp.zeros((CHANNELS, CELLS), f32)
    left = spat_packed[:, :CELLS]
    for y in range(4):
        whole = jnp.concatenate([w_own[y, :, :WIDE], w_other[y, :, :WIDE]], axis=0)
        spatial += dot(whole, cols[y])
        part = dot_nt(left, cols[y])
        for half, ref in ((part[:160], grad_own), (part[160:], grad_other)):
            ref[y, :, :TILE_AT] = half[:, :TILE_AT].astype(bf16)
            ref[y, :, TILE_AT:WIDE] = (half[:, TILE_AT:] + sums).astype(bf16)
    spatial = jnp.where(own_live, spatial, 0.0).astype(bf16)
    spatial = dot(to_plain, spatial).astype(bf16)

    frames[...] = jnp.zeros(frames.shape, bf16)
    for k in range(3):
        for y, at, start, size in pieces_of(k * CHANNELS, (k + 1) * CHANNELS, SPAN_T):
            first = start - k * CHANNELS
            frames[y, at : at + size, k * CELLS : (k + 1) * CELLS] = spatial[first : first + size]
    for y in range(4):
        part = dot_nt(taps[...], frames[y]).astype(bf16)
        grad_own[y, :, WIDE:] = part[:160]
        grad_other[y, :, WIDE:] = part[160:]


def end_kernel(
    place, norm, gain, group, group_row, latent, g_here, pre_grad, terms,
    result, grad_s, grad_t, grad_gain, grad_shift,
):
    height = place[0]
    own_live = (iota((1, CELLS), 1) >> 4) < height
    mean, rstd, positions = norm[:, 0:1], norm[:, 1:2], norm[:1, 2:3]
    scale = lax.rsqrt(positions)
    count = positions * GROUP_SIZE
    total = terms[0].astype(f32)
    for n in range(1, 16):
        total += terms[n].astype(f32)
    scaled = total * scale
    grad_s[...] = scaled[:10, :180]
    grad_t[...] = pltpu.roll(scaled, 76, 1)[:10, :60]
    sums = total[:, :128] + total[:, 128:]
    wide = [jnp.broadcast_to(sums[SPARE + n : SPARE + n + 1], (64, 128)) for n in range(5)]
    wide = jnp.concatenate(wide, axis=0)
    channel = iota((CHANNELS, 128), 0)
    spot = ((channel >> 3) & 7) * 16 + (channel & 7)
    lane = iota((CHANNELS, 128), 1)
    same = group[...] == group_row[...]

    def chan_row(offset):
        column = jnp.sum(jnp.where(lane == spot + offset, wide, 0.0), axis=1, keepdims=True)
        return turned_back(column)

    def over_group(row):
        return jnp.sum(jnp.where(same, gain[...] * row, 0.0), axis=1, keepdims=True) / count

    gain_row = chan_row(0)
    shift_row = chan_row(8)
    grad_gain[...] = gain_row * scale
    grad_shift[...] = shift_row * scale
    normed = (latent[...].astype(f32) - mean) * rstd
    value = g_here[:, :CELLS].astype(f32) + rstd * (
        turned(gain[...]) * pre_grad[...] - over_group(shift_row) - normed * over_group(gain_row)
    )
    result[...] = jnp.where(own_live, value, 0.0).astype(bf16)


def call(kernel, outs, smem=0, scratch=(), inputs=1, flops=0, moved=0, room=16):
    vmem = pl.BlockSpec(memory_space=pltpu.VMEM)
    specs = [pl.BlockSpec(memory_space=pltpu.SMEM)] * smem + [vmem] * (inputs - smem)
    many = isinstance(outs, tuple)
    return pl.pallas_call(
        kernel,
        out_shape=outs,
        in_specs=specs,
        out_specs=tuple(vmem for _ in outs) if many else vmem,
        scratch_shapes=list(scratch),
        compiler_params=pltpu.CompilerParams(vmem_limit_bytes=room << 20),
        cost_estimate=pl.CostEstimate(flops=flops, bytes_accessed=moved, transcendentals=0),
    )


def shape(dims, kind):
    return jax.ShapeDtypeStruct(dims, kind)


def step_by(value, axes, by):
    peers = lax.axis_size(axes)
    pairs = [(i, i + by) for i in range(peers) if 0 <= i + by < peers]
    return lax.ppermute(value, axes, pairs)


def swap_cores(value):
    return lax.ppermute(value, "tile_2", [(0, 1), (1, 0)])


def extended(own, above, below):
    gap = jnp.zeros((CHANNELS, ABOVE - BELOW - COLUMNS), own.dtype)
    return jnp.concatenate([own, below, gap, above], axis=1)


def local(latents, out_grad, w_spatial, w_temporal, norm_gain, norm_shift, heights):
    height = heights[0]
    core = lax.axis_index("tile_2")
    strip = lax.axis_index(TILE)
    place = jnp.stack([height, strip]).astype(jnp.int32)
    live = (jnp.arange(CELLS, dtype=jnp.int32) // COLUMNS < height)[None, :]
    latent = latents[0]
    grad = jnp.where(live, out_grad[0], jnp.zeros((), bf16))

    group = jnp.arange(CHANNELS, dtype=jnp.int32) // GROUP_SIZE
    group_column = group[:, None]

    shard = jnp.concatenate([w_spatial, w_temporal], axis=1)
    shard = jnp.pad(shard, ((0, 6), (0, 16)))
    near = call(
        start_kernel, shape((16, 16, 256), bf16), smem=1, inputs=4, flops=1 << 20, moved=1 << 18
    )(place, latent, group_column, shard)
    near = exchange(near, ROW_Z).reshape(4, 64, 256)
    packed = call(pack_kernel, shape((16, 40, PACK), bf16), flops=1 << 27, moved=3 << 19)(near)
    w_own = exchange(packed, PLANE).reshape(4, 160, PACK)

    both = jnp.stack([latent, grad])
    tall = height == 16
    last = jnp.where(tall, both[:, :, 240:256], both[:, :, 112:128])
    above = step_by(last, TILE, 1)
    below = step_by(both[:, :, :COLUMNS], TILE, -1)
    w_own, above, below = lax.optimization_barrier((w_own, above, below))
    w_other = swap_cores(w_own)
    latent_ext = extended(latent, above[0], below[0])
    grad_ext = extended(grad, above[1], below[1])
    grad_last = step_by(grad_ext, FRAME, 1)
    grad_next = step_by(grad_ext, FRAME, -1)

    packed_row = jnp.arange(CHANNELS, dtype=jnp.int32)
    half, rest = packed_row // 160, packed_row % 160
    order = rest // 40 * 80 + rest % 40 // 10 * 20 + rest % 10
    order = order + jnp.where(half == 0, core, 1 - core) * 10
    gain_row, shift_row = norm_gain[None], norm_shift[None]
    block = shape((4, 160, PACK), bf16)
    grad_own, grad_other, pre_grad, norm = call(
        main_kernel,
        (block, block, shape((CHANNELS, CELLS), f32), shape((CHANNELS, 128), f32)),
        smem=1,
        inputs=12,
        scratch=(
            pltpu.VMEM((4, WIDE, CELLS), bf16),
            pltpu.VMEM((4 * SPAN, CHANNELS), bf16),
            pltpu.VMEM((4 * SPAN_T, CHANNELS), bf16),
            pltpu.VMEM((4, CELLS, 3 * CELLS), bf16),
            pltpu.VMEM((CHANNELS, 3 * CELLS), bf16),
        ),
        flops=5 << 30,
        moved=8 << 20,
        room=28,
    )(
        place, gain_row, shift_row, order[:, None], order[None, :], group_column,
        latent_ext, grad_next, grad_ext, grad_last, w_own, w_other,
    )

    blocks = (16, 40, PACK)
    pair = call(pair_kernel, shape(blocks, bf16), inputs=2, flops=1 << 20, moved=1 << 22)(
        grad_own.reshape(blocks), swap_cores(grad_other).reshape(blocks)
    )
    terms = exchange(pair, PLANE)
    parts = call(unpack_kernel, shape((4, 64, 256), bf16), flops=1 << 27, moved=1 << 21)(terms)
    parts = exchange(parts.reshape(16, 16, 256), ROW_Z)
    grad_input, grad_spatial, grad_temporal, grad_gain, grad_shift = call(
        end_kernel,
        (
            shape((CHANNELS, CELLS), bf16),
            shape((10, 180), f32),
            shape((10, 60), f32),
            shape((1, CHANNELS), f32),
            shape((1, CHANNELS), f32),
        ),
        smem=1,
        inputs=9,
        flops=1 << 22,
        moved=1 << 20,
    )(
        place, norm, gain_row, group_column, group[None, :], latent, grad_ext, pre_grad, parts,
    )
    return grad_input[None], grad_spatial, grad_temporal, grad_gain[0], grad_shift[0]


def solution(mesh):
    split = Mesh(
        mesh.devices.reshape(4, 4, 4, 4, 2), ("frame_0", "frame_1", "tile_0", "tile_1", "tile_2")
    )
    placed = (
        P(FRAME, None, TILE),
        P(FRAME, None, TILE),
        P(TILE, FRAME),
        P(TILE, FRAME),
        P(),
        P(),
        P(TILE),
    )
    return jax.shard_map(
        local,
        mesh=split,
        in_specs=placed,
        out_specs=(P(FRAME, None, TILE), P(TILE, FRAME), P(TILE, FRAME), P(), P()),
        check_vma=False,
    )
```

```python
import functools

import jax
import jax.numpy as jnp
from jax import lax
from jax.experimental import pallas as pl
from jax.experimental.pallas import tpu as pltpu
from jax.sharding import Mesh
from jax.sharding import PartitionSpec as P

GROUPS = 32
GROUP_SIZE = 10
CHANNELS = 320
COLUMNS = 16
STRIPS = 32
FRAMES = 16
CELLS = 256
EXT = 384
BELOW = 256
ABOVE = 368
SPAN = 720
SPAN_T = 240
WIDE = 768
PACK = 1024
EPSILON = 1e-05
SPARE = 10
TILE_AT = 640
FREE = 80

TILE = ("tile_0", "tile_1", "tile_2")
FRAME = ("frame_0", "frame_1")
ROW_Z = ("tile_1", "frame_1")
PLANE = ("frame_0", "tile_0")
PLANE_CORE = ("frame_0", "tile_0", "tile_2")

bf16 = jnp.bfloat16
f32 = jnp.float32
NT = (((1,), (1,)), ((), ()))


def iota(shape, dim):
    return lax.broadcasted_iota(jnp.int32, shape, dim)


def dot(a, b):
    return jnp.dot(a, b, preferred_element_type=f32)


def dot_nt(a, b):
    return lax.dot_general(a, b, NT, preferred_element_type=f32)


def zero_one(mask):
    return jnp.where(mask, 1.0, 0.0).astype(bf16)


def exchange(blocks, axes):
    return lax.all_to_all(blocks, axes, 0, 0, tiled=True)


def column_place(z_low):
    source = iota((256, PACK), 0)
    place = iota((256, PACK), 1)
    spatial = (source < 180) & (place == source + z_low * 180)
    temporal = (source >= 180) & (source < 240)
    temporal &= place == source + (WIDE - 180 + z_low * 60)
    return zero_one(spatial | temporal)


def row_place(shape, dim_small, dim_padded):
    small = iota(shape, dim_small)
    padded = iota(shape, dim_padded)
    match = small < 0
    for a in range(4):
        match |= (small >= 10 * a) & (small < 10 * a + 10) & (padded == small + 6 * a)
    return zero_one(match)


def rounded(value):
    return value.astype(bf16).astype(f32)


def pieces_in(value):
    first = rounded(value)
    second = rounded(value - first)
    return first, second, rounded(value - first - second)


def with_tile(block, tile):
    return jnp.concatenate([block[:, :TILE_AT], tile, block[:, WIDE:]], axis=1)


def start_kernel(place, latent, group, w_spatial, w_temporal, out, left, right):
    height = place[0]
    live = (iota((1, CELLS), 1) >> 4) < height
    value = jnp.where(live, latent[...].astype(f32), 0.0)
    chan_sum = jnp.sum(value, axis=1, keepdims=True)
    chan_square = jnp.sum(value * value, axis=1, keepdims=True)
    lane = iota((CHANNELS, 128), 1)
    terms = jnp.where(lane == group[...], chan_sum, 0.0)
    terms += jnp.where(lane == group[...] + GROUPS, chan_square, 0.0)
    cells = (height * COLUMNS).astype(f32)
    stats = jnp.sum(terms, axis=0, keepdims=True)
    stats += jnp.where(iota((1, 128), 1) == 2 * GROUPS, cells, 0.0)
    row = iota((16, 128), 0)
    extra = jnp.zeros((16, 128), f32)
    for n, piece in enumerate(pieces_in(stats)):
        extra += jnp.where(row == SPARE + n, piece, 0.0)
    extra = jnp.concatenate([extra, jnp.zeros((16, 128), f32)], axis=1)
    left[...] = jnp.zeros((16, 256), f32)
    right[...] = jnp.zeros((16, 256), f32)
    left[:10, :180] = w_spatial[...].astype(f32)
    right[:10, :60] = w_temporal[...].astype(f32)
    block = (left[...] + pltpu.roll(right[...], 180, 1) + extra).astype(bf16)
    for n in range(16):
        out[n] = block


def pack_kernel(blocks, out):
    total = jnp.zeros((64, PACK), f32)
    stats = jnp.zeros((64, 128), f32)
    for z_low in range(4):
        rows = jnp.concatenate([blocks[4 * a + z_low] for a in range(4)], axis=0)
        total += dot(rows, column_place(z_low))
        stats += rows[:, :128].astype(f32)
    packed = dot(row_place((40, 64), 0, 1), total.astype(bf16))
    row = iota((64, 128), 0) & 15
    stats = jnp.where((row >= SPARE) & (row < SPARE + 3), stats, 0.0)
    stats = jnp.sum(stats, axis=0, keepdims=True)
    line = iota((40, 128), 0)
    lane = iota((40, 128), 1)
    wanted = (line, line + GROUPS, 0 * line + 2 * GROUPS)
    tile = packed[:, TILE_AT:WIDE]
    for q in range(3):
        mask = (lane == wanted[q]) & ((line < GROUPS) | (q == 2))
        column = jnp.sum(jnp.where(mask, stats, 0.0), axis=1, keepdims=True)
        for n, piece in enumerate(pieces_in(column)):
            tile += jnp.where(lane == FREE + 3 * q + n, piece, 0.0)
    packed = with_tile(packed, tile).astype(bf16)
    for n in range(16):
        out[n] = packed


def stat_columns(w_own, w_other, group):
    halves = []
    for ref in (w_own, w_other):
        half = jnp.zeros((40, 128), f32)
        for y in range(4):
            tile = ref[y, :, TILE_AT:WIDE].astype(f32).reshape(4, 40, 128)
            half += tile[0] + tile[1] + tile[2] + tile[3]
        halves.append(half)
    total = halves[0] + halves[1]
    line = iota((40, 128), 0)
    lane = iota((40, 128), 1)

    def quantity(q):
        mask = (lane >= FREE + 3 * q) & (lane < FREE + 3 * q + 3)
        return jnp.sum(jnp.where(mask, total, 0.0), axis=1, keepdims=True)

    def pick(q):
        across = jnp.sum(jnp.where(line == lane, quantity(q), 0.0), axis=0, keepdims=True)
        wide = iota((CHANNELS, 128), 1)
        return jnp.sum(jnp.where(wide == group, across, 0.0), axis=1, keepdims=True)

    positions = quantity(2)[:1]
    count = positions * GROUP_SIZE
    mean = pick(0) / count
    rstd = lax.rsqrt(pick(1) / count - mean * mean + EPSILON)
    return positions, mean, rstd


def sums_split(value):
    first = rounded(value)
    return first + pltpu.roll(rounded(value - first), 16, 1)


def sums_joined(tile):
    lane = iota((40, 128), 1)
    mask = (lane >= FREE) & (lane < FREE + 16)
    return jnp.where(mask, tile + pltpu.roll(tile, 112, 1), 0.0)


def pair_kernel(own, other, out):
    lane = iota((40, 128), 1)

    def body(n, _):
        total = own[n].astype(f32) + other[n].astype(f32)
        tile = total[:, TILE_AT:WIDE]
        tile = jnp.where(lane < FREE, tile, sums_split(sums_joined(tile)))
        out[n] = with_tile(total, tile).astype(bf16)
        return 0

    lax.fori_loop(0, 16, body, 0)


def unpack_kernel(terms, out):
    total = terms[0].astype(f32)
    for n in range(1, 16):
        total += terms[n].astype(f32)
    sums = pltpu.roll(sums_joined(total[:, TILE_AT:WIDE]), 128 - FREE, 1)
    for step in (16, 32, 64):
        sums += pltpu.roll(sums, step, 1)
    mine = (iota((40, 128), 1) >> 4) == (iota((40, 128), 0) & 7)
    sums = jnp.sum(jnp.where(mine, sums, 0.0).reshape(5, 8, 128), axis=1)
    first = rounded(sums)
    sums = jnp.concatenate([first, rounded(sums - first)], axis=1)
    row = iota((16, 256), 0)
    extra = jnp.zeros((16, 256), f32)
    for n in range(5):
        extra += jnp.where(row == SPARE + n, sums[n : n + 1], 0.0)
    rows = dot(row_place((64, 40), 1, 0), total.astype(bf16)).astype(bf16)
    for z_low in range(4):
        block = dot_nt(rows, column_place(z_low))
        for a in range(4):
            out[4 * a + z_low] = (block[16 * a : 16 * a + 16] + extra).astype(bf16)


def turned(row):
    eye = iota((CHANNELS, CHANNELS), 0) == iota((CHANNELS, CHANNELS), 1)
    return jnp.sum(jnp.where(eye, row, 0.0), axis=1, keepdims=True)


def turned_back(column):
    eye = iota((CHANNELS, CHANNELS), 0) == iota((CHANNELS, CHANNELS), 1)
    return jnp.sum(jnp.where(eye, column, 0.0), axis=0, keepdims=True)


def pieces_of(start, stop, span):
    while start < stop:
        end = min(stop, (start // span + 1) * span)
        yield start // span, start % span, start, end - start
        start = end


def main_kernel(
    place, gain, shift, order, order_row, group, latent, g_next, g_here, g_last,
    w_own, w_other, grad_own, grad_other, pre_grad, norm, cols, turned_s, turned_t, frames, taps,
):
    height = place[0]
    strip = place[1]
    lane = iota((1, EXT), 1)
    live = ((lane < CELLS) & ((lane >> 4) < height)) | (
        (lane >= BELOW) & (lane < BELOW + COLUMNS) & (strip < STRIPS - 1)
    ) | ((lane >= ABOVE) & (strip > 0))
    to_packed = zero_one(order[...] == iota((CHANNELS, CHANNELS), 1))
    to_plain = zero_one(iota((CHANNELS, CHANNELS), 0) == order_row[...])

    for y in range(4):
        whole = jnp.concatenate([w_own[y], w_other[y]], axis=0)
        across = whole.T
        turned_s[y * SPAN : (y + 1) * SPAN, :] = across[:SPAN]
        turned_t[y * SPAN_T : (y + 1) * SPAN_T, :] = across[WIDE : WIDE + SPAN_T]

    positions, mean, rstd = stat_columns(w_own, w_other, group[...])
    lane_n = iota((CHANNELS, 128), 1)
    norm[...] = jnp.where(lane_n == 0, mean, jnp.where(lane_n == 1, rstd, positions))
    gain_column = turned(gain[...])
    shift_column = turned(shift[...])
    normed = (latent[...].astype(f32) - mean) * rstd
    pre_act = gain_column * normed + shift_column
    sigmoid = 1.0 / (1.0 + jnp.exp(-pre_act))
    active = jnp.where(live, pre_act * sigmoid, 0.0).astype(bf16)

    grad_spat = jnp.zeros((CHANNELS, EXT), f32)
    for k, ref in enumerate((g_next, g_here, g_last)):
        packed = dot(to_packed, ref[...]).astype(bf16)
        taps[:, k * CELLS : (k + 1) * CELLS] = packed[:, :CELLS]
        grad_spat += dot(turned_t[k * CHANNELS : (k + 1) * CHANNELS, :], packed)
    grad_spat = jnp.where(live, grad_spat, 0.0).astype(bf16)
    spat_packed = dot(to_packed, grad_spat).astype(bf16)

    for y in range(4):
        cols[y, SPAN:, :] = jnp.zeros((WIDE - SPAN, CELLS), bf16)
    cell = iota((1, CELLS), 1)
    source = iota((EXT, CELLS), 0)
    grad_act = jnp.zeros((CHANNELS, CELLS), f32)
    for k in range(9):
        row = (cell >> 4) + (k // 3 - 1)
        column = (cell & 15) + (k % 3 - 1)
        base = jnp.where(row < 0, ABOVE, jnp.where(row == height, BELOW, row * COLUMNS))
        wanted = jnp.where((column >= 0) & (column < COLUMNS), base + column, -1)
        move = zero_one(source == wanted)
        moved = dot(active, move).astype(bf16)
        for y, at, start, size in pieces_of(k * CHANNELS, (k + 1) * CHANNELS, SPAN):
            first = start - k * CHANNELS
            cols[y, at : at + size, :] = moved[first : first + size]
        back = 8 - k
        grad_act += dot(
            turned_s[back * CHANNELS : (back + 1) * CHANNELS, :],
            dot(spat_packed, move).astype(bf16),
        )

    own_live = live[:, :CELLS]
    act = pre_act[:, :CELLS]
    sig = sigmoid[:, :CELLS]
    grad_pre = jnp.where(own_live, grad_act * sig * (1.0 + act * (1.0 - sig)), 0.0)
    pre_grad[...] = grad_pre
    chan_gain = jnp.sum(grad_pre * normed[:, :CELLS], axis=1, keepdims=True)
    chan_shift = jnp.sum(grad_pre, axis=1, keepdims=True)
    spot = (iota((CHANNELS, 128), 0) & 7) + FREE
    sums = jnp.where(lane_n == spot, chan_gain, 0.0)
    sums += jnp.where(lane_n == spot + 8, chan_shift, 0.0)
    sums = sums_split(jnp.sum(sums.reshape(40, 8, 128), axis=1))
    sums = jnp.concatenate([sums] * 4, axis=0)

    spatial = jnp.zeros((CHANNELS, CELLS), f32)
    left = spat_packed[:, :CELLS]
    for y in range(4):
        whole = jnp.concatenate([w_own[y, :, :WIDE], w_other[y, :, :WIDE]], axis=0)
        spatial += dot(whole, cols[y])
        part = dot_nt(left, cols[y])
        for half, ref in ((part[:160], grad_own), (part[160:], grad_other)):
            ref[y, :, :TILE_AT] = half[:, :TILE_AT].astype(bf16)
            ref[y, :, TILE_AT:WIDE] = (half[:, TILE_AT:] + sums).astype(bf16)
    spatial = jnp.where(own_live, spatial, 0.0).astype(bf16)
    spatial = dot(to_plain, spatial).astype(bf16)

    frames[...] = jnp.zeros(frames.shape, bf16)
    for k in range(3):
        for y, at, start, size in pieces_of(k * CHANNELS, (k + 1) * CHANNELS, SPAN_T):
            first = start - k * CHANNELS
            frames[y, at : at + size, k * CELLS : (k + 1) * CELLS] = spatial[first : first + size]
    for y in range(4):
        part = dot_nt(taps[...], frames[y]).astype(bf16)
        grad_own[y, :, WIDE:] = part[:160]
        grad_other[y, :, WIDE:] = part[160:]


def end_kernel(
    place, norm, gain, group, group_row, latent, g_here, pre_grad, terms,
    result, grad_s, grad_t, grad_gain, grad_shift,
):
    height = place[0]
    own_live = (iota((1, CELLS), 1) >> 4) < height
    mean, rstd, positions = norm[:, 0:1], norm[:, 1:2], norm[:1, 2:3]
    scale = lax.rsqrt(positions)
    count = positions * GROUP_SIZE
    total = terms[0].astype(f32)
    for n in range(1, 16):
        total += terms[n].astype(f32)
    scaled = total * scale
    grad_s[...] = scaled[:10, :180]
    grad_t[...] = pltpu.roll(scaled, 76, 1)[:10, :60]
    sums = total[:, :128] + total[:, 128:]
    wide = [jnp.broadcast_to(sums[SPARE + n : SPARE + n + 1], (64, 128)) for n in range(5)]
    wide = jnp.concatenate(wide, axis=0)
    channel = iota((CHANNELS, 128), 0)
    spot = ((channel >> 3) & 7) * 16 + (channel & 7)
    lane = iota((CHANNELS, 128), 1)
    same = group[...] == group_row[...]

    def chan_row(offset):
        column = jnp.sum(jnp.where(lane == spot + offset, wide, 0.0), axis=1, keepdims=True)
        return turned_back(column)

    def over_group(row):
        return jnp.sum(jnp.where(same, gain[...] * row, 0.0), axis=1, keepdims=True) / count

    gain_row = chan_row(0)
    shift_row = chan_row(8)
    grad_gain[...] = (gain_row * scale).reshape(CHANNELS)
    grad_shift[...] = (shift_row * scale).reshape(CHANNELS)
    normed = (latent[...].astype(f32) - mean) * rstd
    value = g_here[:, :CELLS].astype(f32) + rstd * (
        turned(gain[...]) * pre_grad[...] - over_group(shift_row) - normed * over_group(gain_row)
    )
    result[...] = jnp.where(own_live, value, 0.0).astype(bf16)


def call(kernel, outs, smem=0, scratch=(), inputs=1, flops=0, moved=0, room=16):
    vmem = pl.BlockSpec(memory_space=pltpu.VMEM)
    specs = [pl.BlockSpec(memory_space=pltpu.SMEM)] * smem + [vmem] * (inputs - smem)
    many = isinstance(outs, tuple)
    return pl.pallas_call(
        kernel,
        out_shape=outs,
        in_specs=specs,
        out_specs=tuple(vmem for _ in outs) if many else vmem,
        scratch_shapes=list(scratch),
        compiler_params=pltpu.CompilerParams(vmem_limit_bytes=room << 20),
        cost_estimate=pl.CostEstimate(flops=flops, bytes_accessed=moved, transcendentals=0),
    )


def shape(dims, kind):
    return jax.ShapeDtypeStruct(dims, kind)


def step_by(value, axes, by):
    peers = lax.axis_size(axes)
    pairs = [(i, i + by) for i in range(peers) if 0 <= i + by < peers]
    return lax.ppermute(value, axes, pairs)


def swap_cores(value):
    return lax.ppermute(value, "tile_2", [(0, 1), (1, 0)])


def extended(own, above, below):
    gap = jnp.zeros((CHANNELS, ABOVE - BELOW - COLUMNS), own.dtype)
    return jnp.concatenate([own, below, gap, above], axis=1)


def local(latents, out_grad, w_spatial, w_temporal, norm_gain, norm_shift, heights):
    height = heights[0]
    core = lax.axis_index("tile_2")
    strip = lax.axis_index(TILE)
    place = jnp.stack([height, strip]).astype(jnp.int32)
    live = (jnp.arange(CELLS, dtype=jnp.int32) // COLUMNS < height)[None, :]
    latent = latents[0]
    grad = jnp.where(live, out_grad[0], jnp.zeros((), bf16))

    group = jnp.arange(CHANNELS, dtype=jnp.int32) // GROUP_SIZE
    group_column = group[:, None]

    near = call(
        start_kernel,
        shape((16, 16, 256), bf16),
        smem=1,
        inputs=5,
        scratch=(pltpu.VMEM((16, 256), f32), pltpu.VMEM((16, 256), f32)),
        flops=1 << 20,
        moved=1 << 18,
    )(place, latent, group_column, w_spatial, w_temporal)
    near = exchange(near, ROW_Z)

    both = jnp.stack([latent, grad])
    tall = height == 16
    last = jnp.where(tall, both[:, :, 240:256], both[:, :, 112:128])
    above = step_by(last, TILE, 1)
    below = step_by(both[:, :, :COLUMNS], TILE, -1)
    near, above, below = lax.optimization_barrier((near, above, below))
    packed = call(pack_kernel, shape((16, 40, PACK), bf16), flops=1 << 27, moved=3 << 19)(
        near
    )
    w_own = exchange(packed, PLANE).reshape(4, 160, PACK)

    latent_ext = extended(latent, above[0], below[0])
    grad_ext = extended(grad, above[1], below[1])
    grad_last = step_by(grad_ext, FRAME, 1)
    grad_next = step_by(grad_ext, FRAME, -1)
    w_own, grad_last, grad_next = lax.optimization_barrier((w_own, grad_last, grad_next))
    w_other = swap_cores(w_own)

    packed_row = jnp.arange(CHANNELS, dtype=jnp.int32)
    half, rest = packed_row // 160, packed_row % 160
    order = rest // 40 * 80 + rest % 40 // 10 * 20 + rest % 10
    order = order + jnp.where(half == 0, core, 1 - core) * 10
    gain_row, shift_row = norm_gain[None], norm_shift[None]
    block = shape((4, 160, PACK), bf16)
    grad_own, grad_other, pre_grad, norm = call(
        main_kernel,
        (block, block, shape((CHANNELS, CELLS), f32), shape((CHANNELS, 128), f32)),
        smem=1,
        inputs=12,
        scratch=(
            pltpu.VMEM((4, WIDE, CELLS), bf16),
            pltpu.VMEM((4 * SPAN, CHANNELS), bf16),
            pltpu.VMEM((4 * SPAN_T, CHANNELS), bf16),
            pltpu.VMEM((4, CELLS, 3 * CELLS), bf16),
            pltpu.VMEM((CHANNELS, 3 * CELLS), bf16),
        ),
        flops=5 << 30,
        moved=8 << 20,
        room=28,
    )(
        place, gain_row, shift_row, order[:, None], order[None, :], group_column,
        latent_ext, grad_next, grad_ext, grad_last, w_own, w_other,
    )

    blocks = (16, 40, PACK)
    pair = call(pair_kernel, shape(blocks, bf16), inputs=2, flops=1 << 20, moved=1 << 22)(
        grad_own.reshape(blocks), swap_cores(grad_other).reshape(blocks)
    )
    terms = exchange(pair, PLANE)
    parts = call(unpack_kernel, shape((16, 16, 256), bf16), flops=1 << 27, moved=1 << 21)(terms)
    parts = exchange(parts, ROW_Z)
    grad_input, grad_spatial, grad_temporal, grad_gain, grad_shift = call(
        end_kernel,
        (
            shape((CHANNELS, CELLS), bf16),
            shape((10, 180), f32),
            shape((10, 60), f32),
            shape((CHANNELS,), f32),
            shape((CHANNELS,), f32),
        ),
        smem=1,
        inputs=9,
        flops=1 << 22,
        moved=1 << 20,
    )(
        place, norm, gain_row, group_column, group[None, :], latent, grad_ext, pre_grad, parts,
    )
    return grad_input[None], grad_spatial, grad_temporal, grad_gain, grad_shift


def solution(mesh):
    split = Mesh(
        mesh.devices.reshape(4, 4, 4, 4, 2), ("frame_0", "frame_1", "tile_0", "tile_1", "tile_2")
    )
    placed = (
        P(FRAME, None, TILE),
        P(FRAME, None, TILE),
        P(TILE, FRAME),
        P(TILE, FRAME),
        P(),
        P(),
        P(TILE),
    )
    return jax.shard_map(
        local,
        mesh=split,
        in_specs=placed,
        out_specs=(P(FRAME, None, TILE), P(TILE, FRAME), P(TILE, FRAME), P(), P()),
        check_vma=False,
    )
```

```python
import jax
import jax.numpy as jnp
from jax import lax
from jax.experimental import pallas as pl
from jax.experimental.pallas import tpu as pltpu
from jax.sharding import Mesh
from jax.sharding import PartitionSpec as P

GROUPS = 32
GROUP_SIZE = 10
CHANNELS = 320
COLUMNS = 16
STRIPS = 32
CELLS = 256
EXT = 384
BELOW = 256
ABOVE = 368
SPAN = 720
SPAN_T = 240
WIDE = 768
PACK = 1024
EPSILON = 1e-05
SPARE = 10
TILE_AT = 640
FREE = 80

TILE = ("tile_0", "tile_1", "tile_2")
FRAME = ("frame_0", "frame_1")
ROW_Z = ("tile_1", "frame_1")
PLANE = ("frame_0", "tile_0")

bf16 = jnp.bfloat16
f32 = jnp.float32
NT = (((1,), (1,)), ((), ()))


def iota(shape, dim):
    return lax.broadcasted_iota(jnp.int32, shape, dim)


def dot(a, b):
    return jnp.dot(a, b, preferred_element_type=f32)


def dot_nt(a, b):
    return lax.dot_general(a, b, NT, preferred_element_type=f32)


def zero_one(mask):
    return jnp.where(mask, 1.0, 0.0).astype(bf16)


def exchange(blocks, axes):
    return lax.all_to_all(blocks, axes, 0, 0, tiled=True)


def column_place(z_low):
    source = iota((256, PACK), 0)
    place = iota((256, PACK), 1)
    spatial = (source < 180) & (place == source + z_low * 180)
    temporal = (source >= 180) & (source < 240)
    temporal &= place == source + (WIDE - 180 + z_low * 60)
    return zero_one(spatial | temporal)


def row_place(shape, dim_small, dim_padded):
    small = iota(shape, dim_small)
    padded = iota(shape, dim_padded)
    match = small < 0
    for a in range(4):
        match |= (small >= 10 * a) & (small < 10 * a + 10) & (padded == small + 6 * a)
    return zero_one(match)


def rounded(value):
    return value.astype(bf16).astype(f32)


def pieces_in(value):
    first = rounded(value)
    second = rounded(value - first)
    return first, second, rounded(value - first - second)


def with_tile(block, tile):
    return jnp.concatenate([block[:, :TILE_AT], tile, block[:, WIDE:]], axis=1)


def start_kernel(place, latent, group, w_spatial, w_temporal, out, left, right):
    height = place[0]
    live = (iota((1, CELLS), 1) >> 4) < height
    value = jnp.where(live, latent[...].astype(f32), 0.0)
    chan_sum = jnp.sum(value, axis=1, keepdims=True)
    chan_square = jnp.sum(value * value, axis=1, keepdims=True)
    lane = iota((CHANNELS, 128), 1)
    terms = jnp.where(lane == group[...], chan_sum, 0.0)
    terms += jnp.where(lane == group[...] + GROUPS, chan_square, 0.0)
    cells = (height * COLUMNS).astype(f32)
    stats = jnp.sum(terms, axis=0, keepdims=True)
    stats += jnp.where(iota((1, 128), 1) == 2 * GROUPS, cells, 0.0)
    row = iota((16, 128), 0)
    extra = jnp.zeros((16, 128), f32)
    for n, piece in enumerate(pieces_in(stats)):
        extra += jnp.where(row == SPARE + n, piece, 0.0)
    extra = jnp.concatenate([extra, jnp.zeros((16, 128), f32)], axis=1)
    left[...] = jnp.zeros((16, 256), f32)
    right[...] = jnp.zeros((16, 256), f32)
    left[:10, :180] = w_spatial[...].astype(f32)
    right[:10, :60] = w_temporal[...].astype(f32)
    block = (left[...] + pltpu.roll(right[...], 180, 1) + extra).astype(bf16)
    for n in range(16):
        out[n] = block


def pack_kernel(blocks, out):
    total = jnp.zeros((64, PACK), f32)
    stats = jnp.zeros((64, 128), f32)
    for z_low in range(4):
        rows = jnp.concatenate([blocks[4 * a + z_low] for a in range(4)], axis=0)
        total += dot(rows, column_place(z_low))
        stats += rows[:, :128].astype(f32)
    packed = dot(row_place((40, 64), 0, 1), total.astype(bf16))
    row = iota((64, 128), 0) & 15
    stats = jnp.where((row >= SPARE) & (row < SPARE + 3), stats, 0.0)
    stats = jnp.sum(stats, axis=0, keepdims=True)
    line = iota((40, 128), 0)
    lane = iota((40, 128), 1)
    wanted = (line, line + GROUPS, 0 * line + 2 * GROUPS)
    tile = packed[:, TILE_AT:WIDE]
    for q in range(3):
        mask = (lane == wanted[q]) & ((line < GROUPS) | (q == 2))
        column = jnp.sum(jnp.where(mask, stats, 0.0), axis=1, keepdims=True)
        for n, piece in enumerate(pieces_in(column)):
            tile += jnp.where(lane == FREE + 3 * q + n, piece, 0.0)
    packed = with_tile(packed, tile).astype(bf16)
    for n in range(16):
        out[n] = packed


def stat_columns(w_own, w_other, group):
    halves = []
    for ref in (w_own, w_other):
        half = jnp.zeros((40, 128), f32)
        for y in range(4):
            tile = ref[y, :, TILE_AT:WIDE].astype(f32).reshape(4, 40, 128)
            half += tile[0] + tile[1] + tile[2] + tile[3]
        halves.append(half)
    total = halves[0] + halves[1]
    line = iota((40, 128), 0)
    lane = iota((40, 128), 1)

    def quantity(q):
        mask = (lane >= FREE + 3 * q) & (lane < FREE + 3 * q + 3)
        return jnp.sum(jnp.where(mask, total, 0.0), axis=1, keepdims=True)

    def pick(q):
        across = jnp.sum(jnp.where(line == lane, quantity(q), 0.0), axis=0, keepdims=True)
        wide = iota((CHANNELS, 128), 1)
        return jnp.sum(jnp.where(wide == group, across, 0.0), axis=1, keepdims=True)

    positions = quantity(2)[:1]
    count = positions * GROUP_SIZE
    mean = pick(0) / count
    rstd = lax.rsqrt(pick(1) / count - mean * mean + EPSILON)
    return positions, mean, rstd


def sums_split(value):
    first = rounded(value)
    return first + pltpu.roll(rounded(value - first), 16, 1)


def sums_joined(tile):
    lane = iota((40, 128), 1)
    mask = (lane >= FREE) & (lane < FREE + 16)
    return jnp.where(mask, tile + pltpu.roll(tile, 112, 1), 0.0)


def pair_kernel(own, other, out):
    lane = iota((40, 128), 1)

    def body(n, _):
        total = own[n].astype(f32) + other[n].astype(f32)
        tile = total[:, TILE_AT:WIDE]
        tile = jnp.where(lane < FREE, tile, sums_split(sums_joined(tile)))
        out[n] = with_tile(total, tile).astype(bf16)
        return 0

    lax.fori_loop(0, 16, body, 0, unroll=4)


def unpack_kernel(terms, out):
    total = terms[0].astype(f32)
    for n in range(1, 16):
        total += terms[n].astype(f32)
    sums = pltpu.roll(sums_joined(total[:, TILE_AT:WIDE]), 128 - FREE, 1)
    for step in (16, 32, 64):
        sums += pltpu.roll(sums, step, 1)
    mine = (iota((40, 128), 1) >> 4) == (iota((40, 128), 0) & 7)
    sums = jnp.sum(jnp.where(mine, sums, 0.0).reshape(5, 8, 128), axis=1)
    first = rounded(sums)
    sums = jnp.concatenate([first, rounded(sums - first)], axis=1)
    row = iota((16, 256), 0)
    extra = jnp.zeros((16, 256), f32)
    for n in range(5):
        extra += jnp.where(row == SPARE + n, sums[n : n + 1], 0.0)
    rows = dot(row_place((64, 40), 1, 0), total.astype(bf16)).astype(bf16)
    for z_low in range(4):
        block = dot_nt(rows, column_place(z_low))
        for a in range(4):
            out[4 * a + z_low] = (block[16 * a : 16 * a + 16] + extra).astype(bf16)


def turned(row):
    eye = iota((CHANNELS, CHANNELS), 0) == iota((CHANNELS, CHANNELS), 1)
    return jnp.sum(jnp.where(eye, row, 0.0), axis=1, keepdims=True)


def turned_back(column):
    eye = iota((CHANNELS, CHANNELS), 0) == iota((CHANNELS, CHANNELS), 1)
    return jnp.sum(jnp.where(eye, column, 0.0), axis=0, keepdims=True)


def pieces_of(start, stop, span):
    while start < stop:
        end = min(stop, (start // span + 1) * span)
        yield start // span, start % span, start, end - start
        start = end


def main_kernel(
    place, gain, shift, order, order_row, group, latent, g_next, g_here, g_last,
    w_own, w_other, grad_own, grad_other, pre_grad, norm, cols, turned_s, turned_t, frames, taps,
):
    height = place[0]
    strip = place[1]
    lane = iota((1, EXT), 1)
    live = ((lane < CELLS) & ((lane >> 4) < height)) | (
        (lane >= BELOW) & (lane < BELOW + COLUMNS) & (strip < STRIPS - 1)
    ) | ((lane >= ABOVE) & (strip > 0))
    to_packed = zero_one(order[...] == iota((CHANNELS, CHANNELS), 1))
    to_plain = zero_one(iota((CHANNELS, CHANNELS), 0) == order_row[...])

    for y in range(4):
        whole = jnp.concatenate([w_own[y], w_other[y]], axis=0)
        across = whole.T
        turned_s[y * SPAN : (y + 1) * SPAN, :] = across[:SPAN]
        turned_t[y * SPAN_T : (y + 1) * SPAN_T, :] = across[WIDE : WIDE + SPAN_T]

    positions, mean, rstd = stat_columns(w_own, w_other, group[...])
    lane_n = iota((CHANNELS, 128), 1)
    norm[...] = jnp.where(lane_n == 0, mean, jnp.where(lane_n == 1, rstd, positions))
    gain_column = turned(gain[...])
    shift_column = turned(shift[...])
    normed = (latent[...].astype(f32) - mean) * rstd
    pre_act = gain_column * normed + shift_column
    sigmoid = 1.0 / (1.0 + jnp.exp(-pre_act))
    active = jnp.where(live, pre_act * sigmoid, 0.0).astype(bf16)

    grad_spat = jnp.zeros((CHANNELS, EXT), f32)
    for k, ref in enumerate((g_next, g_here, g_last)):
        packed = dot(to_packed, ref[...]).astype(bf16)
        taps[:, k * CELLS : (k + 1) * CELLS] = packed[:, :CELLS]
        grad_spat += dot(turned_t[k * CHANNELS : (k + 1) * CHANNELS, :], packed)
    grad_spat = jnp.where(live, grad_spat, 0.0).astype(bf16)
    spat_packed = dot(to_packed, grad_spat).astype(bf16)

    for y in range(4):
        cols[y, SPAN:, :] = jnp.zeros((WIDE - SPAN, CELLS), bf16)
    cell = iota((1, CELLS), 1)
    source = iota((EXT, CELLS), 0)
    grad_act = jnp.zeros((CHANNELS, CELLS), f32)
    for k in range(9):
        row = (cell >> 4) + (k // 3 - 1)
        column = (cell & 15) + (k % 3 - 1)
        base = jnp.where(row < 0, ABOVE, jnp.where(row == height, BELOW, row * COLUMNS))
        wanted = jnp.where((column >= 0) & (column < COLUMNS), base + column, -1)
        move = zero_one(source == wanted)
        moved = dot(active, move).astype(bf16)
        for y, at, start, size in pieces_of(k * CHANNELS, (k + 1) * CHANNELS, SPAN):
            first = start - k * CHANNELS
            cols[y, at : at + size, :] = moved[first : first + size]
        back = 8 - k
        grad_act += dot(
            turned_s[back * CHANNELS : (back + 1) * CHANNELS, :],
            dot(spat_packed, move).astype(bf16),
        )

    own_live = live[:, :CELLS]
    act = pre_act[:, :CELLS]
    sig = sigmoid[:, :CELLS]
    grad_pre = jnp.where(own_live, grad_act * sig * (1.0 + act * (1.0 - sig)), 0.0)
    pre_grad[...] = grad_pre
    chan_gain = jnp.sum(grad_pre * normed[:, :CELLS], axis=1, keepdims=True)
    chan_shift = jnp.sum(grad_pre, axis=1, keepdims=True)
    spot = (iota((CHANNELS, 128), 0) & 7) + FREE
    sums = jnp.where(lane_n == spot, chan_gain, 0.0)
    sums += jnp.where(lane_n == spot + 8, chan_shift, 0.0)
    sums = sums_split(jnp.sum(sums.reshape(40, 8, 128), axis=1))
    sums = jnp.concatenate([sums] * 4, axis=0)

    spatial = jnp.zeros((CHANNELS, CELLS), f32)
    left = spat_packed[:, :CELLS]
    for y in range(4):
        whole = jnp.concatenate([w_own[y, :, :WIDE], w_other[y, :, :WIDE]], axis=0)
        spatial += dot(whole, cols[y])
        part = dot_nt(left, cols[y])
        for half, ref in ((part[:160], grad_own), (part[160:], grad_other)):
            ref[y, :, :TILE_AT] = half[:, :TILE_AT].astype(bf16)
            ref[y, :, TILE_AT:WIDE] = (half[:, TILE_AT:] + sums).astype(bf16)
    spatial = jnp.where(own_live, spatial, 0.0).astype(bf16)
    spatial = dot(to_plain, spatial).astype(bf16)

    frames[...] = jnp.zeros(frames.shape, bf16)
    for k in range(3):
        for y, at, start, size in pieces_of(k * CHANNELS, (k + 1) * CHANNELS, SPAN_T):
            first = start - k * CHANNELS
            frames[y, at : at + size, k * CELLS : (k + 1) * CELLS] = spatial[first : first + size]
    for y in range(4):
        part = dot_nt(taps[...], frames[y]).astype(bf16)
        grad_own[y, :, WIDE:] = part[:160]
        grad_other[y, :, WIDE:] = part[160:]


def end_kernel(
    place, norm, gain, group, latent, g_here, pre_grad, terms,
    result, grad_s, grad_t, grad_gain, grad_shift,
):
    height = place[0]
    own_live = (iota((1, CELLS), 1) >> 4) < height
    mean, rstd, positions = norm[:, 0:1], norm[:, 1:2], norm[:1, 2:3]
    scale = lax.rsqrt(positions)
    count = positions * GROUP_SIZE
    total = terms[0].astype(f32)
    for n in range(1, 16):
        total += terms[n].astype(f32)
    scaled = total * scale
    grad_s[...] = scaled[:10, :180]
    grad_t[...] = pltpu.roll(scaled, 76, 1)[:10, :60]
    sums = total[:, :128] + total[:, 128:]
    wide = [jnp.broadcast_to(sums[SPARE + n : SPARE + n + 1], (64, 128)) for n in range(5)]
    wide = jnp.concatenate(wide, axis=0)
    channel = iota((CHANNELS, 128), 0)
    spot = ((channel >> 3) & 7) * 16 + (channel & 7)
    lane = iota((CHANNELS, 128), 1)
    eye = iota((CHANNELS, CHANNELS), 0) == iota((CHANNELS, CHANNELS), 1)
    same = group[...] == jnp.sum(jnp.where(eye, group[...], 0), axis=0, keepdims=True)

    def chan_row(offset):
        column = jnp.sum(jnp.where(lane == spot + offset, wide, 0.0), axis=1, keepdims=True)
        return turned_back(column)

    def over_group(row):
        return jnp.sum(jnp.where(same, gain[...] * row, 0.0), axis=1, keepdims=True) / count

    gain_row = chan_row(0)
    shift_row = chan_row(8)
    grad_gain[...] = (gain_row * scale).reshape(CHANNELS)
    grad_shift[...] = (shift_row * scale).reshape(CHANNELS)
    normed = (latent[...].astype(f32) - mean) * rstd
    value = g_here[:, :CELLS].astype(f32) + rstd * (
        turned(gain[...]) * pre_grad[...] - over_group(shift_row) - normed * over_group(gain_row)
    )
    result[...] = jnp.where(own_live, value, 0.0).astype(bf16)


def call(kernel, outs, smem=0, scratch=(), inputs=1, flops=0, moved=0, room=16):
    vmem = pl.BlockSpec(memory_space=pltpu.VMEM)
    specs = [pl.BlockSpec(memory_space=pltpu.SMEM)] * smem + [vmem] * (inputs - smem)
    many = isinstance(outs, tuple)
    return pl.pallas_call(
        kernel,
        out_shape=outs,
        in_specs=specs,
        out_specs=tuple(vmem for _ in outs) if many else vmem,
        scratch_shapes=list(scratch),
        compiler_params=pltpu.CompilerParams(vmem_limit_bytes=room << 20),
        cost_estimate=pl.CostEstimate(flops=flops, bytes_accessed=moved, transcendentals=0),
    )


def shape(dims, kind):
    return jax.ShapeDtypeStruct(dims, kind)


def step_by(value, axes, by):
    peers = lax.axis_size(axes)
    pairs = [(i, i + by) for i in range(peers) if 0 <= i + by < peers]
    return lax.ppermute(value, axes, pairs)


def swap_cores(value):
    return lax.ppermute(value, "tile_2", [(0, 1), (1, 0)])


def extended(own, above, below):
    gap = jnp.zeros((CHANNELS, ABOVE - BELOW - COLUMNS), own.dtype)
    return jnp.concatenate([own, below, gap, above], axis=1)


def local(latents, out_grad, w_spatial, w_temporal, norm_gain, norm_shift, heights):
    height = heights[0]
    core = lax.axis_index("tile_2")
    strip = lax.axis_index(TILE)
    place = jnp.stack([height, strip]).astype(jnp.int32)
    live = (jnp.arange(CELLS, dtype=jnp.int32) // COLUMNS < height)[None, :]
    latent = latents[0]
    grad = jnp.where(live, out_grad[0], jnp.zeros((), bf16))

    group = jnp.arange(CHANNELS, dtype=jnp.int32) // GROUP_SIZE
    group_column = group[:, None]

    near = call(
        start_kernel,
        shape((16, 16, 256), bf16),
        smem=1,
        inputs=5,
        scratch=(pltpu.VMEM((16, 256), f32), pltpu.VMEM((16, 256), f32)),
        flops=1 << 20,
        moved=1 << 18,
    )(place, latent, group_column, w_spatial, w_temporal)
    near = exchange(near, ROW_Z)

    both = jnp.stack([latent, grad])
    tall = height == 16
    last = jnp.where(tall, both[:, :, 240:256], both[:, :, 112:128])
    above = step_by(last, TILE, 1)
    below = step_by(both[:, :, :COLUMNS], TILE, -1)
    near, above, below = lax.optimization_barrier((near, above, below))
    packed = call(pack_kernel, shape((16, 40, PACK), bf16), flops=1 << 27, moved=3 << 19)(
        near
    )
    w_own = exchange(packed, PLANE).reshape(4, 160, PACK)

    latent_ext = extended(latent, above[0], below[0])
    grad_ext = extended(grad, above[1], below[1])
    grad_last = step_by(grad_ext, FRAME, 1)
    grad_next = step_by(grad_ext, FRAME, -1)
    w_own, grad_last, grad_next = lax.optimization_barrier((w_own, grad_last, grad_next))
    w_other = swap_cores(w_own)

    packed_row = jnp.arange(CHANNELS, dtype=jnp.int32)
    half, rest = packed_row // 160, packed_row % 160
    order = rest // 40 * 80 + rest % 40 // 10 * 20 + rest % 10
    order = order + jnp.where(half == 0, core, 1 - core) * 10
    gain_row, shift_row = norm_gain[None], norm_shift[None]
    block = shape((4, 160, PACK), bf16)
    grad_own, grad_other, pre_grad, norm = call(
        main_kernel,
        (block, block, shape((CHANNELS, CELLS), f32), shape((CHANNELS, 128), f32)),
        smem=1,
        inputs=12,
        scratch=(
            pltpu.VMEM((4, WIDE, CELLS), bf16),
            pltpu.VMEM((4 * SPAN, CHANNELS), bf16),
            pltpu.VMEM((4 * SPAN_T, CHANNELS), bf16),
            pltpu.VMEM((4, CELLS, 3 * CELLS), bf16),
            pltpu.VMEM((CHANNELS, 3 * CELLS), bf16),
        ),
        flops=5 << 30,
        moved=8 << 20,
        room=28,
    )(
        place, gain_row, shift_row, order[:, None], order[None, :], group_column,
        latent_ext, grad_next, grad_ext, grad_last, w_own, w_other,
    )

    blocks = (16, 40, PACK)
    pair = call(pair_kernel, shape(blocks, bf16), inputs=2, flops=1 << 20, moved=1 << 22)(
        grad_own.reshape(blocks), swap_cores(grad_other).reshape(blocks)
    )
    terms = exchange(pair, PLANE)
    parts = call(unpack_kernel, shape((16, 16, 256), bf16), flops=1 << 27, moved=1 << 21)(terms)
    parts = exchange(parts, ROW_Z)
    grad_input, grad_spatial, grad_temporal, grad_gain, grad_shift = call(
        end_kernel,
        (
            shape((CHANNELS, CELLS), bf16),
            shape((10, 180), f32),
            shape((10, 60), f32),
            shape((CHANNELS,), f32),
            shape((CHANNELS,), f32),
        ),
        smem=1,
        inputs=8,
        flops=1 << 22,
        moved=1 << 20,
    )(
        place, norm, gain_row, group_column, latent, grad_ext, pre_grad, parts,
    )
    return grad_input[None], grad_spatial, grad_temporal, grad_gain, grad_shift


def solution(mesh):
    split = Mesh(
        mesh.devices.reshape(4, 4, 4, 4, 2), ("frame_0", "frame_1", "tile_0", "tile_1", "tile_2")
    )
    placed = (
        P(FRAME, None, TILE),
        P(FRAME, None, TILE),
        P(TILE, FRAME),
        P(TILE, FRAME),
        P(),
        P(),
        P(TILE),
    )
    return jax.shard_map(
        local,
        mesh=split,
        in_specs=placed,
        out_specs=(P(FRAME, None, TILE), P(TILE, FRAME), P(TILE, FRAME), P(), P()),
        check_vma=False,
    )
```

```python
import jax
import jax.numpy as jnp
from jax import lax
from jax.experimental import pallas as pl
from jax.experimental.pallas import tpu as pltpu
from jax.sharding import Mesh
from jax.sharding import PartitionSpec as P

GROUPS = 32
GROUP_SIZE = 10
CHANNELS = 320
COLUMNS = 16
STRIPS = 32
CELLS = 256
EXT = 384
BELOW = 256
ABOVE = 368
SPAN = 720
SPAN_T = 240
WIDE = 768
PACK = 1024
EPSILON = 1e-05
SPARE = 10
TILE_AT = 640
FREE = 80

TILE = ("tile_0", "tile_1", "tile_2")
FRAME = ("frame_0", "frame_1")
ROW_Z = ("tile_1", "frame_1")
PLANE = ("frame_0", "tile_0")

bf16 = jnp.bfloat16
f32 = jnp.float32
NT = (((1,), (1,)), ((), ()))


def iota(shape, dim):
    return lax.broadcasted_iota(jnp.int32, shape, dim)


def dot(a, b):
    return jnp.dot(a, b, preferred_element_type=f32)


def dot_nt(a, b):
    return lax.dot_general(a, b, NT, preferred_element_type=f32)


def zero_one(mask):
    return jnp.where(mask, 1.0, 0.0).astype(bf16)


def exchange(blocks, axes):
    return lax.all_to_all(blocks, axes, 0, 0, tiled=True)


def column_place(z_low):
    source = iota((256, PACK), 0)
    place = iota((256, PACK), 1)
    spatial = (source < 180) & (place == source + z_low * 180)
    temporal = (source >= 180) & (source < 240)
    temporal &= place == source + (WIDE - 180 + z_low * 60)
    return zero_one(spatial | temporal)


def row_place(shape, dim_small, dim_padded):
    small = iota(shape, dim_small)
    padded = iota(shape, dim_padded)
    match = small < 0
    for a in range(4):
        match |= (small >= 10 * a) & (small < 10 * a + 10) & (padded == small + 6 * a)
    return zero_one(match)


def rounded(value):
    return value.astype(bf16).astype(f32)


def pieces_in(value):
    first = rounded(value)
    second = rounded(value - first)
    return first, second, rounded(value - first - second)


def with_tile(block, tile):
    return jnp.concatenate([block[:, :TILE_AT], tile, block[:, WIDE:]], axis=1)


def fetched(pairs, sems):
    copies = [pltpu.make_async_copy(a, b, sems.at[n]) for n, (a, b) in enumerate(pairs)]
    for copy in copies:
        copy.start()
    for copy in copies:
        copy.wait()


def start_kernel(
    place, group, latent_at, grad_at, w_spatial_at, w_temporal_at, out, masked,
    latent, grad, w_spatial, w_temporal, left, right, sems,
):
    fetched(
        (
            (latent_at, latent),
            (grad_at, grad),
            (w_spatial_at, w_spatial),
            (w_temporal_at, w_temporal),
        ),
        sems,
    )
    height = place[0]
    live = (iota((1, CELLS), 1) >> 4) < height
    masked[...] = jnp.where(live, grad[...].astype(f32), 0.0).astype(bf16)
    value = jnp.where(live, latent[...].astype(f32), 0.0)
    chan_sum = jnp.sum(value, axis=1, keepdims=True)
    chan_square = jnp.sum(value * value, axis=1, keepdims=True)
    lane = iota((CHANNELS, 128), 1)
    terms = jnp.where(lane == group[...], chan_sum, 0.0)
    terms += jnp.where(lane == group[...] + GROUPS, chan_square, 0.0)
    cells = (height * COLUMNS).astype(f32)
    stats = jnp.sum(terms, axis=0, keepdims=True)
    stats += jnp.where(iota((1, 128), 1) == 2 * GROUPS, cells, 0.0)
    row = iota((16, 128), 0)
    extra = jnp.zeros((16, 128), f32)
    for n, piece in enumerate(pieces_in(stats)):
        extra += jnp.where(row == SPARE + n, piece, 0.0)
    extra = jnp.concatenate([extra, jnp.zeros((16, 128), f32)], axis=1)
    left[...] = jnp.zeros((16, 256), f32)
    right[...] = jnp.zeros((16, 256), f32)
    left[:10, :180] = w_spatial[...].astype(f32)
    right[:10, :60] = w_temporal[...].astype(f32)
    block = (left[...] + pltpu.roll(right[...], 180, 1) + extra).astype(bf16)
    for n in range(16):
        out[n] = block


def row_move(set_index, first):
    cell = iota((CELLS, 128), 0)
    lane = iota((CELLS, 128), 1)
    inside = (lane >> 4) == set_index
    return zero_one(inside & (cell == first + (lane & 15)))


def rows_kernel(place, latent, g_next, g_here, g_last, row_first, row_last):
    last = (place[0] - 1) * COLUMNS
    head = jnp.zeros((CHANNELS, 128), f32)
    tail = jnp.zeros((CHANNELS, 128), f32)
    for n, ref in enumerate((latent, g_next, g_here, g_last)):
        head += dot(ref[...], row_move(n, 0))
        tail += dot(ref[...], row_move(n, last))
    row_first[...] = head.astype(bf16)
    row_last[...] = tail.astype(bf16)


def pack_kernel(blocks, out):
    total = jnp.zeros((64, PACK), f32)
    stats = jnp.zeros((64, 128), f32)
    for z_low in range(4):
        rows = jnp.concatenate([blocks[4 * a + z_low] for a in range(4)], axis=0)
        total += dot(rows, column_place(z_low))
        stats += rows[:, :128].astype(f32)
    packed = dot(row_place((40, 64), 0, 1), total.astype(bf16))
    row = iota((64, 128), 0) & 15
    stats = jnp.where((row >= SPARE) & (row < SPARE + 3), stats, 0.0)
    stats = jnp.sum(stats, axis=0, keepdims=True)
    line = iota((40, 128), 0)
    lane = iota((40, 128), 1)
    wanted = (line, line + GROUPS, 0 * line + 2 * GROUPS)
    tile = packed[:, TILE_AT:WIDE]
    for q in range(3):
        mask = (lane == wanted[q]) & ((line < GROUPS) | (q == 2))
        column = jnp.sum(jnp.where(mask, stats, 0.0), axis=1, keepdims=True)
        for n, piece in enumerate(pieces_in(column)):
            tile += jnp.where(lane == FREE + 3 * q + n, piece, 0.0)
    packed = with_tile(packed, tile).astype(bf16)
    for n in range(16):
        out[n] = packed


def stat_columns(w_own, w_other, group):
    halves = []
    for ref in (w_own, w_other):
        half = jnp.zeros((40, 128), f32)
        for y in range(4):
            tile = ref[y, :, TILE_AT:WIDE].astype(f32).reshape(4, 40, 128)
            half += tile[0] + tile[1] + tile[2] + tile[3]
        halves.append(half)
    total = halves[0] + halves[1]
    line = iota((40, 128), 0)
    lane = iota((40, 128), 1)

    def quantity(q):
        mask = (lane >= FREE + 3 * q) & (lane < FREE + 3 * q + 3)
        return jnp.sum(jnp.where(mask, total, 0.0), axis=1, keepdims=True)

    def pick(q):
        across = jnp.sum(jnp.where(line == lane, quantity(q), 0.0), axis=0, keepdims=True)
        wide = iota((CHANNELS, 128), 1)
        return jnp.sum(jnp.where(wide == group, across, 0.0), axis=1, keepdims=True)

    positions = quantity(2)[:1]
    count = positions * GROUP_SIZE
    mean = pick(0) / count
    rstd = lax.rsqrt(pick(1) / count - mean * mean + EPSILON)
    return positions, mean, rstd


def sums_split(value):
    first = rounded(value)
    return first + pltpu.roll(rounded(value - first), 16, 1)


def sums_joined(tile):
    lane = iota((40, 128), 1)
    mask = (lane >= FREE) & (lane < FREE + 16)
    return jnp.where(mask, tile + pltpu.roll(tile, 112, 1), 0.0)


def pair_kernel(own, other, out):
    lane = iota((40, 128), 1)

    def body(n, _):
        total = own[n].astype(f32) + other[n].astype(f32)
        tile = total[:, TILE_AT:WIDE]
        tile = jnp.where(lane < FREE, tile, sums_split(sums_joined(tile)))
        out[n] = with_tile(total, tile).astype(bf16)
        return 0

    lax.fori_loop(0, 16, body, 0, unroll=4)


def unpack_kernel(terms, out):
    total = terms[0].astype(f32)
    for n in range(1, 16):
        total += terms[n].astype(f32)
    sums = pltpu.roll(sums_joined(total[:, TILE_AT:WIDE]), 128 - FREE, 1)
    for step in (16, 32, 64):
        sums += pltpu.roll(sums, step, 1)
    mine = (iota((40, 128), 1) >> 4) == (iota((40, 128), 0) & 7)
    sums = jnp.sum(jnp.where(mine, sums, 0.0).reshape(5, 8, 128), axis=1)
    first = rounded(sums)
    sums = jnp.concatenate([first, rounded(sums - first)], axis=1)
    row = iota((16, 256), 0)
    extra = jnp.zeros((16, 256), f32)
    for n in range(5):
        extra += jnp.where(row == SPARE + n, sums[n : n + 1], 0.0)
    rows = dot(row_place((64, 40), 1, 0), total.astype(bf16)).astype(bf16)
    for z_low in range(4):
        block = dot_nt(rows, column_place(z_low))
        for a in range(4):
            out[4 * a + z_low] = (block[16 * a : 16 * a + 16] + extra).astype(bf16)


def turned(row):
    eye = iota((CHANNELS, CHANNELS), 0) == iota((CHANNELS, CHANNELS), 1)
    return jnp.sum(jnp.where(eye, row, 0.0), axis=1, keepdims=True)


def turned_back(column):
    eye = iota((CHANNELS, CHANNELS), 0) == iota((CHANNELS, CHANNELS), 1)
    return jnp.sum(jnp.where(eye, column, 0.0), axis=0, keepdims=True)


def pieces_of(start, stop, span):
    while start < stop:
        end = min(stop, (start // span + 1) * span)
        yield start // span, start % span, start, end - start
        start = end


def main_kernel(
    place, gain, shift, order, order_row, group, latent_own, g_here,
    above_at, below_at, g_next_at, g_last_at, w_own, w_other, grad_own, grad_other, pre_grad, norm, cols, turned_s, turned_t, frames, taps,
    g_next, g_last, above, below, sems,
):
    copies = (
        pltpu.make_async_copy(g_next_at, g_next, sems.at[0]),
        pltpu.make_async_copy(g_last_at, g_last, sems.at[1]),
        pltpu.make_async_copy(above_at, above, sems.at[2]),
        pltpu.make_async_copy(below_at, below, sems.at[3]),
    )
    for copy in copies:
        copy.start()
    height = place[0]
    strip = place[1]

    def extended(own, set_index):
        source = iota((128, 128), 0)
        lane = iota((128, 128), 1)
        from_set = (source >> 4) == set_index
        low = from_set & (lane == (source & 15))
        high = from_set & (lane == (source & 15) + (ABOVE - BELOW))
        rows = dot(below[...], zero_one(low)) + dot(above[...], zero_one(high))
        return jnp.concatenate([own, rows.astype(bf16)], axis=1)

    lane = iota((1, EXT), 1)
    live = ((lane < CELLS) & ((lane >> 4) < height)) | (
        (lane >= BELOW) & (lane < BELOW + COLUMNS) & (strip < STRIPS - 1)
    ) | ((lane >= ABOVE) & (strip > 0))
    to_packed = zero_one(order[...] == iota((CHANNELS, CHANNELS), 1))
    to_plain = zero_one(iota((CHANNELS, CHANNELS), 0) == order_row[...])

    for y in range(4):
        whole = jnp.concatenate([w_own[y], w_other[y]], axis=0)
        across = whole.T
        turned_s[y * SPAN : (y + 1) * SPAN, :] = across[:SPAN]
        turned_t[y * SPAN_T : (y + 1) * SPAN_T, :] = across[WIDE : WIDE + SPAN_T]

    for copy in copies:
        copy.wait()
    positions, mean, rstd = stat_columns(w_own, w_other, group[...])
    lane_n = iota((CHANNELS, 128), 1)
    norm[...] = jnp.where(lane_n == 0, mean, jnp.where(lane_n == 1, rstd, positions))
    gain_column = turned(gain[...])
    shift_column = turned(shift[...])
    normed = (extended(latent_own[...], 0).astype(f32) - mean) * rstd
    pre_act = gain_column * normed + shift_column
    sigmoid = 1.0 / (1.0 + jnp.exp(-pre_act))
    active = jnp.where(live, pre_act * sigmoid, 0.0).astype(bf16)

    grad_spat = jnp.zeros((CHANNELS, EXT), f32)
    for k, ref in enumerate((g_next, g_here, g_last)):
        packed = dot(to_packed, extended(ref[...], 1 + k)).astype(bf16)
        taps[:, k * CELLS : (k + 1) * CELLS] = packed[:, :CELLS]
        grad_spat += dot(turned_t[k * CHANNELS : (k + 1) * CHANNELS, :], packed)
    grad_spat = jnp.where(live, grad_spat, 0.0).astype(bf16)
    spat_packed = dot(to_packed, grad_spat).astype(bf16)

    for y in range(4):
        cols[y, SPAN:, :] = jnp.zeros((WIDE - SPAN, CELLS), bf16)
    cell = iota((1, CELLS), 1)
    source = iota((EXT, CELLS), 0)
    grad_act = jnp.zeros((CHANNELS, CELLS), f32)
    for k in range(9):
        row = (cell >> 4) + (k // 3 - 1)
        column = (cell & 15) + (k % 3 - 1)
        base = jnp.where(row < 0, ABOVE, jnp.where(row == height, BELOW, row * COLUMNS))
        wanted = jnp.where((column >= 0) & (column < COLUMNS), base + column, -1)
        move = zero_one(source == wanted)
        moved = dot(active, move).astype(bf16)
        for y, at, start, size in pieces_of(k * CHANNELS, (k + 1) * CHANNELS, SPAN):
            first = start - k * CHANNELS
            cols[y, at : at + size, :] = moved[first : first + size]
        back = 8 - k
        grad_act += dot(
            turned_s[back * CHANNELS : (back + 1) * CHANNELS, :],
            dot(spat_packed, move).astype(bf16),
        )

    own_live = live[:, :CELLS]
    act = pre_act[:, :CELLS]
    sig = sigmoid[:, :CELLS]
    grad_pre = jnp.where(own_live, grad_act * sig * (1.0 + act * (1.0 - sig)), 0.0)
    pre_grad[...] = grad_pre
    chan_gain = jnp.sum(grad_pre * normed[:, :CELLS], axis=1, keepdims=True)
    chan_shift = jnp.sum(grad_pre, axis=1, keepdims=True)
    spot = (iota((CHANNELS, 128), 0) & 7) + FREE
    sums = jnp.where(lane_n == spot, chan_gain, 0.0)
    sums += jnp.where(lane_n == spot + 8, chan_shift, 0.0)
    sums = sums_split(jnp.sum(sums.reshape(40, 8, 128), axis=1))
    sums = jnp.concatenate([sums] * 4, axis=0)

    spatial = jnp.zeros((CHANNELS, CELLS), f32)
    left = spat_packed[:, :CELLS]
    for y in range(4):
        whole = jnp.concatenate([w_own[y, :, :WIDE], w_other[y, :, :WIDE]], axis=0)
        spatial += dot(whole, cols[y])
        part = dot_nt(left, cols[y])
        for half, ref in ((part[:160], grad_own), (part[160:], grad_other)):
            ref[y, :, :TILE_AT] = half[:, :TILE_AT].astype(bf16)
            ref[y, :, TILE_AT:WIDE] = (half[:, TILE_AT:] + sums).astype(bf16)
    spatial = jnp.where(own_live, spatial, 0.0).astype(bf16)
    spatial = dot(to_plain, spatial).astype(bf16)

    frames[...] = jnp.zeros(frames.shape, bf16)
    for k in range(3):
        for y, at, start, size in pieces_of(k * CHANNELS, (k + 1) * CHANNELS, SPAN_T):
            first = start - k * CHANNELS
            frames[y, at : at + size, k * CELLS : (k + 1) * CELLS] = spatial[first : first + size]
    for y in range(4):
        part = dot_nt(taps[...], frames[y]).astype(bf16)
        grad_own[y, :, WIDE:] = part[:160]
        grad_other[y, :, WIDE:] = part[160:]


def end_kernel(
    place, norm, gain, group, latent, g_here, pre_grad, terms,
    result, grad_s, grad_t, grad_gain, grad_shift,
):
    height = place[0]
    own_live = (iota((1, CELLS), 1) >> 4) < height
    mean, rstd, positions = norm[:, 0:1], norm[:, 1:2], norm[:1, 2:3]
    scale = lax.rsqrt(positions)
    count = positions * GROUP_SIZE
    total = terms[0].astype(f32)
    for n in range(1, 16):
        total += terms[n].astype(f32)
    scaled = total * scale
    grad_s[...] = scaled[:10, :180]
    grad_t[...] = pltpu.roll(scaled, 76, 1)[:10, :60]
    sums = total[:, :128] + total[:, 128:]
    wide = [jnp.broadcast_to(sums[SPARE + n : SPARE + n + 1], (64, 128)) for n in range(5)]
    wide = jnp.concatenate(wide, axis=0)
    channel = iota((CHANNELS, 128), 0)
    spot = ((channel >> 3) & 7) * 16 + (channel & 7)
    lane = iota((CHANNELS, 128), 1)
    eye = iota((CHANNELS, CHANNELS), 0) == iota((CHANNELS, CHANNELS), 1)
    same = group[...] == jnp.sum(jnp.where(eye, group[...], 0), axis=0, keepdims=True)

    def chan_row(offset):
        column = jnp.sum(jnp.where(lane == spot + offset, wide, 0.0), axis=1, keepdims=True)
        return turned_back(column)

    def over_group(row):
        return jnp.sum(jnp.where(same, gain[...] * row, 0.0), axis=1, keepdims=True) / count

    gain_row = chan_row(0)
    shift_row = chan_row(8)
    grad_gain[...] = (gain_row * scale).reshape(CHANNELS)
    grad_shift[...] = (shift_row * scale).reshape(CHANNELS)
    normed = (latent[...].astype(f32) - mean) * rstd
    value = g_here[...].astype(f32) + rstd * (
        turned(gain[...]) * pre_grad[...] - over_group(shift_row) - normed * over_group(gain_row)
    )
    result[...] = jnp.where(own_live, value, 0.0).astype(bf16)


def call(kernel, outs, smem=0, scratch=(), inputs=1, apart=0, space=pltpu.HBM, flops=0, moved=0, room=16):
    vmem = pl.BlockSpec(memory_space=pltpu.VMEM)
    specs = [pl.BlockSpec(memory_space=pltpu.SMEM)] * smem + [vmem] * (inputs - smem)
    for n in range(*apart) if apart else ():
        specs[n] = pl.BlockSpec(memory_space=space)
    many = isinstance(outs, tuple)
    return pl.pallas_call(
        kernel,
        out_shape=outs,
        in_specs=specs,
        out_specs=tuple(vmem for _ in outs) if many else vmem,
        scratch_shapes=list(scratch),
        compiler_params=pltpu.CompilerParams(vmem_limit_bytes=room << 20),
        cost_estimate=pl.CostEstimate(flops=flops, bytes_accessed=moved, transcendentals=0),
    )


def shape(dims, kind):
    return jax.ShapeDtypeStruct(dims, kind)


def step_by(value, axes, by):
    peers = lax.axis_size(axes)
    pairs = [(i, i + by) for i in range(peers) if 0 <= i + by < peers]
    return lax.ppermute(value, axes, pairs)


def swap_cores(value):
    return lax.ppermute(value, "tile_2", [(0, 1), (1, 0)])


def local(latents, out_grad, w_spatial, w_temporal, norm_gain, norm_shift, heights):
    height = heights[0]
    core = lax.axis_index("tile_2")
    place = jnp.stack([height, lax.axis_index(TILE)]).astype(jnp.int32)
    latent = latents[0]
    group = jnp.arange(CHANNELS, dtype=jnp.int32) // GROUP_SIZE
    group_column = group[:, None]
    field = (CHANNELS, CELLS)

    near, grad = call(
        start_kernel,
        (shape((16, 16, 256), bf16), shape(field, bf16)),
        smem=1,
        inputs=6,
        apart=(2, 6),
        scratch=(
            pltpu.VMEM(field, bf16),
            pltpu.VMEM(field, bf16),
            pltpu.VMEM((10, 180), bf16),
            pltpu.VMEM((10, 60), bf16),
            pltpu.VMEM((16, 256), f32),
            pltpu.VMEM((16, 256), f32),
            pltpu.SemaphoreType.DMA((4,)),
        ),
        flops=1 << 20,
        moved=1 << 18,
        room=58,
    )(place, group_column, latent, out_grad[0], w_spatial, w_temporal)

    grad_last = step_by(grad, FRAME, 1)
    grad_next = step_by(grad, FRAME, -1)
    near = exchange(near, ROW_Z)
    packed = call(pack_kernel, shape((16, 40, PACK), bf16), flops=1 << 27, moved=3 << 19)(near)
    w_own = exchange(packed, PLANE).reshape(4, 160, PACK)

    row_tile = shape((CHANNELS, 128), bf16)
    row_first, row_last = call(
        rows_kernel, (row_tile, row_tile), smem=1, inputs=5, flops=1 << 28, moved=1 << 20
    )(place, latent, grad_next, grad, grad_last)
    above = step_by(row_last, TILE, 1)
    below = step_by(row_first, TILE, -1)
    w_own, above, below = lax.optimization_barrier((w_own, above, below))
    w_other = swap_cores(w_own)

    packed_row = jnp.arange(CHANNELS, dtype=jnp.int32)
    half, rest = packed_row // 160, packed_row % 160
    order = rest // 40 * 80 + rest % 40 // 10 * 20 + rest % 10
    order = order + jnp.where(half == 0, core, 1 - core) * 10
    gain_row, shift_row = norm_gain[None], norm_shift[None]
    block = shape((4, 160, PACK), bf16)
    grad_own, grad_other, pre_grad, norm = call(
        main_kernel,
        (block, block, shape((CHANNELS, CELLS), f32), shape((CHANNELS, 128), f32)),
        smem=1,
        inputs=14,
        apart=(8, 12),
        space=pl.ANY,
        scratch=(
            pltpu.VMEM((4, WIDE, CELLS), bf16),
            pltpu.VMEM((4 * SPAN, CHANNELS), bf16),
            pltpu.VMEM((4 * SPAN_T, CHANNELS), bf16),
            pltpu.VMEM((4, CELLS, 3 * CELLS), bf16),
            pltpu.VMEM((CHANNELS, 3 * CELLS), bf16),
            pltpu.VMEM(field, bf16),
            pltpu.VMEM(field, bf16),
            pltpu.VMEM((CHANNELS, 128), bf16),
            pltpu.VMEM((CHANNELS, 128), bf16),
            pltpu.SemaphoreType.DMA((4,)),
        ),
        flops=5 << 30,
        moved=8 << 20,
        room=28,
    )(
        place, gain_row, shift_row, order[:, None], order[None, :], group_column,
        latent, grad, above, below, grad_next, grad_last, w_own, w_other,
    )

    blocks = (16, 40, PACK)
    pair = call(pair_kernel, shape(blocks, bf16), inputs=2, flops=1 << 20, moved=1 << 22)(
        grad_own.reshape(blocks), swap_cores(grad_other).reshape(blocks)
    )
    terms = exchange(pair, PLANE)
    parts = call(unpack_kernel, shape((16, 16, 256), bf16), flops=1 << 27, moved=1 << 21)(terms)
    parts = exchange(parts, ROW_Z)
    grad_input, grad_spatial, grad_temporal, grad_gain, grad_shift = call(
        end_kernel,
        (
            shape((CHANNELS, CELLS), bf16),
            shape((10, 180), f32),
            shape((10, 60), f32),
            shape((CHANNELS,), f32),
            shape((CHANNELS,), f32),
        ),
        smem=1,
        inputs=8,
        flops=1 << 22,
        moved=1 << 20,
    )(
        place, norm, gain_row, group_column, latent, grad, pre_grad, parts,
    )
    return grad_input[None], grad_spatial, grad_temporal, grad_gain, grad_shift


def solution(mesh):
    split = Mesh(
        mesh.devices.reshape(4, 4, 4, 4, 2), ("frame_0", "frame_1", "tile_0", "tile_1", "tile_2")
    )
    placed = (
        P(FRAME, None, TILE),
        P(FRAME, None, TILE),
        P(TILE, FRAME),
        P(TILE, FRAME),
        P(),
        P(),
        P(TILE),
    )
    return jax.shard_map(
        local,
        mesh=split,
        in_specs=placed,
        out_specs=(P(FRAME, None, TILE), P(TILE, FRAME), P(TILE, FRAME), P(), P()),
        check_vma=False,
    )
```

```python
import jax
import jax.numpy as jnp
from jax import lax
from jax.experimental import pallas as pl
from jax.experimental.pallas import tpu as pltpu
from jax.sharding import Mesh
from jax.sharding import PartitionSpec as P

GROUPS = 32
GROUP_SIZE = 10
CHANNELS = 320
COLUMNS = 16
STRIPS = 32
CELLS = 256
EXT = 384
BELOW = 256
ABOVE = 368
SPAN = 720
SPAN_T = 240
WIDE = 768
PACK = 1024
EPSILON = 1e-05
SPARE = 10
TILE_AT = 640
FREE = 80

TILE = ("tile_0", "tile_1", "tile_2")
FRAME = ("frame_0", "frame_1")
ROW_Z = ("tile_1", "frame_1")
PLANE = ("frame_0", "tile_0")

bf16 = jnp.bfloat16
f32 = jnp.float32
NT = (((1,), (1,)), ((), ()))


def iota(shape, dim):
    return lax.broadcasted_iota(jnp.int32, shape, dim)


def group_of(dims, dim):
    return (iota(dims, dim) * 6554) >> 16


def dot(a, b):
    return jnp.dot(a, b, preferred_element_type=f32)


def dot_nt(a, b):
    return lax.dot_general(a, b, NT, preferred_element_type=f32)


def zero_one(mask):
    return jnp.where(mask, 1.0, 0.0).astype(bf16)


def exchange(blocks, axes):
    return lax.all_to_all(blocks, axes, 0, 0, tiled=True)


def column_place(z_low):
    source = iota((256, PACK), 0)
    place = iota((256, PACK), 1)
    spatial = (source < 180) & (place == source + z_low * 180)
    temporal = (source >= 180) & (source < 240)
    temporal &= place == source + (WIDE - 180 + z_low * 60)
    return zero_one(spatial | temporal)


def row_place(shape, dim_small, dim_padded):
    small = iota(shape, dim_small)
    padded = iota(shape, dim_padded)
    match = small < 0
    for a in range(4):
        match |= (small >= 10 * a) & (small < 10 * a + 10) & (padded == small + 6 * a)
    return zero_one(match)


def rounded(value):
    return value.astype(bf16).astype(f32)


def pieces_in(value):
    first = rounded(value)
    second = rounded(value - first)
    return first, second, rounded(value - first - second)


def with_tile(block, tile):
    return jnp.concatenate([block[:, :TILE_AT], tile, block[:, WIDE:]], axis=1)


def fetched(pairs, sems):
    copies = [pltpu.make_async_copy(a, b, sems.at[n]) for n, (a, b) in enumerate(pairs)]
    for copy in copies:
        copy.start()
    for copy in copies:
        copy.wait()


def start_kernel(
    place, latent_at, grad_at, w_spatial_at, w_temporal_at, out, masked,
    latent, grad, w_spatial, w_temporal, left, right, sems,
):
    fetched(
        (
            (latent_at, latent),
            (grad_at, grad),
            (w_spatial_at, w_spatial),
            (w_temporal_at, w_temporal),
        ),
        sems,
    )
    height = place[0]
    live = (iota((1, CELLS), 1) >> 4) < height
    masked[...] = jnp.where(live, grad[...].astype(f32), 0.0).astype(bf16)
    value = jnp.where(live, latent[...].astype(f32), 0.0)
    chan_sum = jnp.sum(value, axis=1, keepdims=True)
    chan_square = jnp.sum(value * value, axis=1, keepdims=True)
    lane = iota((CHANNELS, 128), 1)
    group = group_of((CHANNELS, 128), 0)
    terms = jnp.where(lane == group, chan_sum, 0.0)
    terms += jnp.where(lane == group + GROUPS, chan_square, 0.0)
    cells = (height * COLUMNS).astype(f32)
    stats = jnp.sum(terms, axis=0, keepdims=True)
    stats += jnp.where(iota((1, 128), 1) == 2 * GROUPS, cells, 0.0)
    row = iota((16, 128), 0)
    extra = jnp.zeros((16, 128), f32)
    for n, piece in enumerate(pieces_in(stats)):
        extra += jnp.where(row == SPARE + n, piece, 0.0)
    extra = jnp.concatenate([extra, jnp.zeros((16, 128), f32)], axis=1)
    left[...] = jnp.zeros((16, 256), f32)
    right[...] = jnp.zeros((16, 256), f32)
    left[:10, :180] = w_spatial[...].astype(f32)
    right[:10, :60] = w_temporal[...].astype(f32)
    block = (left[...] + pltpu.roll(right[...], 180, 1) + extra).astype(bf16)
    for n in range(16):
        out[n] = block


def row_move(set_index, first):
    cell = iota((CELLS, 128), 0)
    lane = iota((CELLS, 128), 1)
    inside = (lane >> 4) == set_index
    return zero_one(inside & (cell == first + (lane & 15)))


def rows_kernel(place, latent, g_next, g_here, g_last, row_first, row_last):
    last = (place[0] - 1) * COLUMNS
    head = jnp.zeros((CHANNELS, 128), f32)
    tail = jnp.zeros((CHANNELS, 128), f32)
    for n, ref in enumerate((latent, g_next, g_here, g_last)):
        head += dot(ref[...], row_move(n, 0))
        tail += dot(ref[...], row_move(n, last))
    row_first[...] = head.astype(bf16)
    row_last[...] = tail.astype(bf16)


def pack_kernel(blocks, out):
    total = jnp.zeros((64, PACK), f32)
    stats = jnp.zeros((64, 128), f32)
    for z_low in range(4):
        rows = jnp.concatenate([blocks[4 * a + z_low] for a in range(4)], axis=0)
        total += dot(rows, column_place(z_low))
        stats += rows[:, :128].astype(f32)
    packed = dot(row_place((40, 64), 0, 1), total.astype(bf16))
    row = iota((64, 128), 0) & 15
    stats = jnp.where((row >= SPARE) & (row < SPARE + 3), stats, 0.0)
    stats = jnp.sum(stats, axis=0, keepdims=True)
    line = iota((40, 128), 0)
    lane = iota((40, 128), 1)
    wanted = (line, line + GROUPS, 0 * line + 2 * GROUPS)
    tile = packed[:, TILE_AT:WIDE]
    for q in range(3):
        mask = (lane == wanted[q]) & ((line < GROUPS) | (q == 2))
        column = jnp.sum(jnp.where(mask, stats, 0.0), axis=1, keepdims=True)
        for n, piece in enumerate(pieces_in(column)):
            tile += jnp.where(lane == FREE + 3 * q + n, piece, 0.0)
    packed = with_tile(packed, tile).astype(bf16)
    for n in range(16):
        out[n] = packed


def stat_columns(w_own, w_other):
    halves = []
    for ref in (w_own, w_other):
        half = jnp.zeros((40, 128), f32)
        for y in range(4):
            tile = ref[y, :, TILE_AT:WIDE].astype(f32).reshape(4, 40, 128)
            half += tile[0] + tile[1] + tile[2] + tile[3]
        halves.append(half)
    total = halves[0] + halves[1]
    line = iota((40, 128), 0)
    lane = iota((40, 128), 1)

    def quantity(q):
        mask = (lane >= FREE + 3 * q) & (lane < FREE + 3 * q + 3)
        return jnp.sum(jnp.where(mask, total, 0.0), axis=1, keepdims=True)

    def pick(q):
        across = jnp.sum(jnp.where(line == lane, quantity(q), 0.0), axis=0, keepdims=True)
        wide = iota((CHANNELS, 128), 1)
        group = group_of((CHANNELS, 128), 0)
        return jnp.sum(jnp.where(wide == group, across, 0.0), axis=1, keepdims=True)

    positions = quantity(2)[:1]
    count = positions * GROUP_SIZE
    mean = pick(0) / count
    rstd = lax.rsqrt(pick(1) / count - mean * mean + EPSILON)
    return positions, mean, rstd


def sums_split(value):
    first = rounded(value)
    return first + pltpu.roll(rounded(value - first), 16, 1)


def sums_joined(tile):
    lane = iota((40, 128), 1)
    mask = (lane >= FREE) & (lane < FREE + 16)
    return jnp.where(mask, tile + pltpu.roll(tile, 112, 1), 0.0)


def pair_kernel(own, other, out):
    lane = iota((40, 128), 1)

    def body(n, _):
        total = own[n].astype(f32) + other[n].astype(f32)
        tile = total[:, TILE_AT:WIDE]
        tile = jnp.where(lane < FREE, tile, sums_split(sums_joined(tile)))
        out[n] = with_tile(total, tile).astype(bf16)
        return 0

    lax.fori_loop(0, 16, body, 0, unroll=4)


def unpack_kernel(terms, out):
    total = terms[0].astype(f32)
    for n in range(1, 16):
        total += terms[n].astype(f32)
    sums = pltpu.roll(sums_joined(total[:, TILE_AT:WIDE]), 128 - FREE, 1)
    for step in (16, 32, 64):
        sums += pltpu.roll(sums, step, 1)
    mine = (iota((40, 128), 1) >> 4) == (iota((40, 128), 0) & 7)
    sums = jnp.sum(jnp.where(mine, sums, 0.0).reshape(5, 8, 128), axis=1)
    first = rounded(sums)
    sums = jnp.concatenate([first, rounded(sums - first)], axis=1)
    row = iota((16, 256), 0)
    extra = jnp.zeros((16, 256), f32)
    for n in range(5):
        extra += jnp.where(row == SPARE + n, sums[n : n + 1], 0.0)
    rows = dot(row_place((64, 40), 1, 0), total.astype(bf16)).astype(bf16)
    for z_low in range(4):
        block = dot_nt(rows, column_place(z_low))
        for a in range(4):
            out[4 * a + z_low] = (block[16 * a : 16 * a + 16] + extra).astype(bf16)


def turned(row):
    eye = iota((CHANNELS, CHANNELS), 0) == iota((CHANNELS, CHANNELS), 1)
    return jnp.sum(jnp.where(eye, row, 0.0), axis=1, keepdims=True)


def turned_back(column):
    eye = iota((CHANNELS, CHANNELS), 0) == iota((CHANNELS, CHANNELS), 1)
    return jnp.sum(jnp.where(eye, column, 0.0), axis=0, keepdims=True)


def pieces_of(start, stop, span):
    while start < stop:
        end = min(stop, (start // span + 1) * span)
        yield start // span, start % span, start, end - start
        start = end


def ready_kernel(
    place, order, latent, g_here, above, below, g_next, g_last, latent_ext, packed, moves
):
    height = place[0]
    to_packed = zero_one(order[...] == iota((CHANNELS, CHANNELS), 1))

    def extended(own, set_index):
        source = iota((128, 128), 0)
        lane = iota((128, 128), 1)
        from_set = (source >> 4) == set_index
        low = from_set & (lane == (source & 15))
        high = from_set & (lane == (source & 15) + (ABOVE - BELOW))
        rows = dot(below[...], zero_one(low)) + dot(above[...], zero_one(high))
        return jnp.concatenate([own, rows.astype(bf16)], axis=1)

    latent_ext[...] = extended(latent[...], 0)
    for k, ref in enumerate((g_next, g_here, g_last)):
        packed[k] = dot(to_packed, extended(ref[...], 1 + k)).astype(bf16)
    cell = iota((1, CELLS), 1)
    source = iota((EXT, CELLS), 0)
    for k in range(9):
        row = (cell >> 4) + (k // 3 - 1)
        column = (cell & 15) + (k % 3 - 1)
        base = jnp.where(row < 0, ABOVE, jnp.where(row == height, BELOW, row * COLUMNS))
        wanted = jnp.where((column >= 0) & (column < COLUMNS), base + column, -1)
        moves[k] = zero_one(source == wanted)


def main_kernel(
    place, gain, shift, order, order_row, latent, packed, moves, w_own, w_other,
    grad_own, grad_other, pre_grad, norm, cols, turned_s, turned_t, frames, taps,
):
    height = place[0]
    strip = place[1]

    lane = iota((1, EXT), 1)
    live = ((lane < CELLS) & ((lane >> 4) < height)) | (
        (lane >= BELOW) & (lane < BELOW + COLUMNS) & (strip < STRIPS - 1)
    ) | ((lane >= ABOVE) & (strip > 0))
    to_packed = zero_one(order[...] == iota((CHANNELS, CHANNELS), 1))
    to_plain = zero_one(iota((CHANNELS, CHANNELS), 0) == order_row[...])

    for y in range(4):
        whole = jnp.concatenate([w_own[y], w_other[y]], axis=0)
        across = whole.T
        turned_s[y * SPAN : (y + 1) * SPAN, :] = across[:SPAN]
        turned_t[y * SPAN_T : (y + 1) * SPAN_T, :] = across[WIDE : WIDE + SPAN_T]

    positions, mean, rstd = stat_columns(w_own, w_other)
    lane_n = iota((CHANNELS, 128), 1)
    norm[...] = jnp.where(lane_n == 0, mean, jnp.where(lane_n == 1, rstd, positions))
    gain_column = turned(gain[...])
    shift_column = turned(shift[...])
    normed = (latent[...].astype(f32) - mean) * rstd
    pre_act = gain_column * normed + shift_column
    sigmoid = 1.0 / (1.0 + jnp.exp(-pre_act))
    active = jnp.where(live, pre_act * sigmoid, 0.0).astype(bf16)

    grad_spat = jnp.zeros((CHANNELS, EXT), f32)
    for k in range(3):
        taps[:, k * CELLS : (k + 1) * CELLS] = packed[k, :, :CELLS]
        grad_spat += dot(turned_t[k * CHANNELS : (k + 1) * CHANNELS, :], packed[k])
    grad_spat = jnp.where(live, grad_spat, 0.0).astype(bf16)
    spat_packed = dot(to_packed, grad_spat).astype(bf16)

    for y in range(4):
        cols[y, SPAN:, :] = jnp.zeros((WIDE - SPAN, CELLS), bf16)
    grad_act = jnp.zeros((CHANNELS, CELLS), f32)
    for k in range(9):
        move = moves[k]
        moved = dot(active, move).astype(bf16)
        for y, at, start, size in pieces_of(k * CHANNELS, (k + 1) * CHANNELS, SPAN):
            first = start - k * CHANNELS
            cols[y, at : at + size, :] = moved[first : first + size]
        back = 8 - k
        grad_act += dot(
            turned_s[back * CHANNELS : (back + 1) * CHANNELS, :],
            dot(spat_packed, move).astype(bf16),
        )

    own_live = live[:, :CELLS]
    act = pre_act[:, :CELLS]
    sig = sigmoid[:, :CELLS]
    grad_pre = jnp.where(own_live, grad_act * sig * (1.0 + act * (1.0 - sig)), 0.0)
    pre_grad[...] = grad_pre
    chan_gain = jnp.sum(grad_pre * normed[:, :CELLS], axis=1, keepdims=True)
    chan_shift = jnp.sum(grad_pre, axis=1, keepdims=True)
    spot = (iota((CHANNELS, 128), 0) & 7) + FREE
    sums = jnp.where(lane_n == spot, chan_gain, 0.0)
    sums += jnp.where(lane_n == spot + 8, chan_shift, 0.0)
    sums = sums_split(jnp.sum(sums.reshape(40, 8, 128), axis=1))
    sums = jnp.concatenate([sums] * 4, axis=0)

    spatial = jnp.zeros((CHANNELS, CELLS), f32)
    left = spat_packed[:, :CELLS]
    for y in range(4):
        whole = jnp.concatenate([w_own[y, :, :WIDE], w_other[y, :, :WIDE]], axis=0)
        spatial += dot(whole, cols[y])
        part = dot_nt(left, cols[y])
        for half, ref in ((part[:160], grad_own), (part[160:], grad_other)):
            ref[y, :, :TILE_AT] = half[:, :TILE_AT].astype(bf16)
            ref[y, :, TILE_AT:WIDE] = (half[:, TILE_AT:] + sums).astype(bf16)
    spatial = jnp.where(own_live, spatial, 0.0).astype(bf16)
    spatial = dot(to_plain, spatial).astype(bf16)

    frames[...] = jnp.zeros(frames.shape, bf16)
    for k in range(3):
        for y, at, start, size in pieces_of(k * CHANNELS, (k + 1) * CHANNELS, SPAN_T):
            first = start - k * CHANNELS
            frames[y, at : at + size, k * CELLS : (k + 1) * CELLS] = spatial[first : first + size]
    for y in range(4):
        part = dot_nt(taps[...], frames[y]).astype(bf16)
        grad_own[y, :, WIDE:] = part[:160]
        grad_other[y, :, WIDE:] = part[160:]


def end_kernel(
    place, norm, gain, latent, g_here, pre_grad, terms,
    result, grad_s, grad_t, grad_gain, grad_shift,
):
    height = place[0]
    own_live = (iota((1, CELLS), 1) >> 4) < height
    mean, rstd, positions = norm[:, 0:1], norm[:, 1:2], norm[:1, 2:3]
    scale = lax.rsqrt(positions)
    count = positions * GROUP_SIZE
    total = terms[0].astype(f32)
    for n in range(1, 16):
        total += terms[n].astype(f32)
    scaled = total * scale
    grad_s[...] = scaled[:10, :180]
    grad_t[...] = pltpu.roll(scaled, 76, 1)[:10, :60]
    sums = total[:, :128] + total[:, 128:]
    wide = [jnp.broadcast_to(sums[SPARE + n : SPARE + n + 1], (64, 128)) for n in range(5)]
    wide = jnp.concatenate(wide, axis=0)
    channel = iota((CHANNELS, 128), 0)
    spot = ((channel >> 3) & 7) * 16 + (channel & 7)
    lane = iota((CHANNELS, 128), 1)
    square = (CHANNELS, CHANNELS)
    same = group_of(square, 0) == group_of(square, 1)

    def chan_row(offset):
        column = jnp.sum(jnp.where(lane == spot + offset, wide, 0.0), axis=1, keepdims=True)
        return turned_back(column)

    def over_group(row):
        return jnp.sum(jnp.where(same, gain[...] * row, 0.0), axis=1, keepdims=True) / count

    gain_row = chan_row(0)
    shift_row = chan_row(8)
    grad_gain[...] = (gain_row * scale).reshape(CHANNELS)
    grad_shift[...] = (shift_row * scale).reshape(CHANNELS)
    normed = (latent[...].astype(f32) - mean) * rstd
    value = g_here[...].astype(f32) + rstd * (
        turned(gain[...]) * pre_grad[...] - over_group(shift_row) - normed * over_group(gain_row)
    )
    result[...] = jnp.where(own_live, value, 0.0).astype(bf16)


def call(kernel, outs, smem=0, scratch=(), inputs=1, apart=0, space=pltpu.HBM, flops=0, moved=0, room=16):
    vmem = pl.BlockSpec(memory_space=pltpu.VMEM)
    specs = [pl.BlockSpec(memory_space=pltpu.SMEM)] * smem + [vmem] * (inputs - smem)
    for n in range(*apart) if apart else ():
        specs[n] = pl.BlockSpec(memory_space=space)
    many = isinstance(outs, tuple)
    return pl.pallas_call(
        kernel,
        out_shape=outs,
        in_specs=specs,
        out_specs=tuple(vmem for _ in outs) if many else vmem,
        scratch_shapes=list(scratch),
        compiler_params=pltpu.CompilerParams(vmem_limit_bytes=room << 20),
        cost_estimate=pl.CostEstimate(flops=flops, bytes_accessed=moved, transcendentals=0),
    )


def shape(dims, kind):
    return jax.ShapeDtypeStruct(dims, kind)


def step_by(value, axes, by):
    peers = lax.axis_size(axes)
    pairs = [(i, i + by) for i in range(peers) if 0 <= i + by < peers]
    return lax.ppermute(value, axes, pairs)


def swap_cores(value):
    return lax.ppermute(value, "tile_2", [(0, 1), (1, 0)])


def local(latents, out_grad, w_spatial, w_temporal, norm_gain, norm_shift, heights):
    height = heights[0]
    core = lax.axis_index("tile_2")
    place = jnp.stack([height, lax.axis_index(TILE)]).astype(jnp.int32)
    latent = latents[0]
    field = (CHANNELS, CELLS)

    near, grad = call(
        start_kernel,
        (shape((16, 16, 256), bf16), shape(field, bf16)),
        smem=1,
        inputs=5,
        apart=(1, 5),
        scratch=(
            pltpu.VMEM(field, bf16),
            pltpu.VMEM(field, bf16),
            pltpu.VMEM((10, 180), bf16),
            pltpu.VMEM((10, 60), bf16),
            pltpu.VMEM((16, 256), f32),
            pltpu.VMEM((16, 256), f32),
            pltpu.SemaphoreType.DMA((4,)),
        ),
        flops=1 << 20,
        moved=1 << 18,
        room=58,
    )(heights, latent, out_grad[0], w_spatial, w_temporal)

    grad_last = step_by(grad, FRAME, 1)
    grad_next = step_by(grad, FRAME, -1)
    near = exchange(near, ROW_Z)
    packed = call(pack_kernel, shape((16, 40, PACK), bf16), flops=1 << 27, moved=3 << 19)(near)
    w_own = exchange(packed, PLANE).reshape(4, 160, PACK)

    row_tile = shape((CHANNELS, 128), bf16)
    row_first, row_last = call(
        rows_kernel, (row_tile, row_tile), smem=1, inputs=5, flops=1 << 28, moved=1 << 20
    )(place, latent, grad_next, grad, grad_last)
    above = step_by(row_last, TILE, 1)
    below = step_by(row_first, TILE, -1)
    w_own, above, below = lax.optimization_barrier((w_own, above, below))
    w_other = swap_cores(w_own)

    packed_row = jnp.arange(CHANNELS, dtype=jnp.int32)
    half, rest = packed_row // 160, packed_row % 160
    order = rest // 40 * 80 + rest % 40 // 10 * 20 + rest % 10
    order = order + jnp.where(half == 0, core, 1 - core) * 10
    gain_row, shift_row = norm_gain[None], norm_shift[None]
    latent_ext, packed_grad, moves = call(
        ready_kernel,
        (
            shape((CHANNELS, EXT), bf16),
            shape((3, CHANNELS, EXT), bf16),
            shape((9, EXT, CELLS), bf16),
        ),
        smem=1,
        inputs=8,
        flops=1 << 29,
        moved=1 << 21,
    )(place, order[:, None], latent, grad, above, below, grad_next, grad_last)
    block = shape((4, 160, PACK), bf16)
    grad_own, grad_other, pre_grad, norm = call(
        main_kernel,
        (block, block, shape((CHANNELS, CELLS), f32), shape((CHANNELS, 128), f32)),
        smem=1,
        inputs=10,
        scratch=(
            pltpu.VMEM((4, WIDE, CELLS), bf16),
            pltpu.VMEM((4 * SPAN, CHANNELS), bf16),
            pltpu.VMEM((4 * SPAN_T, CHANNELS), bf16),
            pltpu.VMEM((4, CELLS, 3 * CELLS), bf16),
            pltpu.VMEM((CHANNELS, 3 * CELLS), bf16),
        ),
        flops=5 << 30,
        moved=8 << 20,
        room=28,
    )(
        place, gain_row, shift_row, order[:, None], order[None, :], latent_ext,
        packed_grad, moves, w_own, w_other,
    )

    blocks = (16, 40, PACK)
    pair = call(pair_kernel, shape(blocks, bf16), inputs=2, flops=1 << 20, moved=1 << 22)(
        grad_own.reshape(blocks), swap_cores(grad_other).reshape(blocks)
    )
    terms = exchange(pair, PLANE)
    parts = call(unpack_kernel, shape((16, 16, 256), bf16), flops=1 << 27, moved=1 << 21)(terms)
    parts = exchange(parts, ROW_Z)
    grad_input, grad_spatial, grad_temporal, grad_gain, grad_shift = call(
        end_kernel,
        (
            shape((CHANNELS, CELLS), bf16),
            shape((10, 180), f32),
            shape((10, 60), f32),
            shape((CHANNELS,), f32),
            shape((CHANNELS,), f32),
        ),
        smem=1,
        inputs=7,
        flops=1 << 22,
        moved=1 << 20,
    )(
        place, norm, gain_row, latent, grad, pre_grad, parts,
    )
    return grad_input[None], grad_spatial, grad_temporal, grad_gain, grad_shift


def solution(mesh):
    split = Mesh(
        mesh.devices.reshape(4, 4, 4, 4, 2), ("frame_0", "frame_1", "tile_0", "tile_1", "tile_2")
    )
    placed = (
        P(FRAME, None, TILE),
        P(FRAME, None, TILE),
        P(TILE, FRAME),
        P(TILE, FRAME),
        P(),
        P(),
        P(TILE),
    )
    return jax.shard_map(
        local,
        mesh=split,
        in_specs=placed,
        out_specs=(P(FRAME, None, TILE), P(TILE, FRAME), P(TILE, FRAME), P(), P()),
        check_vma=False,
    )
```

```python
import jax
import jax.numpy as jnp
from jax import lax
from jax.experimental import pallas as pl
from jax.experimental.pallas import tpu as pltpu
from jax.sharding import Mesh
from jax.sharding import PartitionSpec as P

GROUPS = 32
GROUP_SIZE = 10
CHANNELS = 320
COLUMNS = 16
STRIPS = 32
CELLS = 256
EXT = 384
BELOW = 256
ABOVE = 368
SPAN = 720
SPAN_T = 240
WIDE = 768
PACK = 1024
EPSILON = 1e-05
SPARE = 10
TILE_AT = 640
FREE = 80

TILE = ("tile_0", "tile_1", "tile_2")
FRAME = ("frame_0", "frame_1")
ROW_Z = ("tile_1", "frame_1")
PLANE = ("frame_0", "tile_0")

bf16 = jnp.bfloat16
f32 = jnp.float32
NT = (((1,), (1,)), ((), ()))


def iota(shape, dim):
    return lax.broadcasted_iota(jnp.int32, shape, dim)


def group_of(dims, dim):
    return (iota(dims, dim) * 6554) >> 16


def dot(a, b):
    return jnp.dot(a, b, preferred_element_type=f32)


def dot_nt(a, b):
    return lax.dot_general(a, b, NT, preferred_element_type=f32)


def zero_one(mask):
    return jnp.where(mask, 1.0, 0.0).astype(bf16)


def exchange(blocks, axes):
    return lax.all_to_all(blocks, axes, 0, 0, tiled=True)


def column_place(z_low):
    source = iota((256, PACK), 0)
    place = iota((256, PACK), 1)
    spatial = (source < 180) & (place == source + z_low * 180)
    temporal = (source >= 180) & (source < 240)
    temporal &= place == source + (WIDE - 180 + z_low * 60)
    return zero_one(spatial | temporal)


def row_place(shape, dim_small, dim_padded):
    small = iota(shape, dim_small)
    padded = iota(shape, dim_padded)
    match = small < 0
    for a in range(4):
        match |= (small >= 10 * a) & (small < 10 * a + 10) & (padded == small + 6 * a)
    return zero_one(match)


def rounded(value):
    return value.astype(bf16).astype(f32)


def pieces_in(value):
    first = rounded(value)
    second = rounded(value - first)
    return first, second, rounded(value - first - second)


def with_tile(block, tile):
    return jnp.concatenate([block[:, :TILE_AT], tile, block[:, WIDE:]], axis=1)


def fetched(pairs, sems):
    copies = [pltpu.make_async_copy(a, b, sems.at[n]) for n, (a, b) in enumerate(pairs)]
    for copy in copies:
        copy.start()
    for copy in copies:
        copy.wait()


def start_kernel(
    place, latent_at, grad_at, w_spatial_at, w_temporal_at, out, masked,
    latent, grad, w_spatial, w_temporal, left, right, sems,
):
    fetched(
        (
            (latent_at, latent),
            (grad_at, grad),
            (w_spatial_at, w_spatial),
            (w_temporal_at, w_temporal),
        ),
        sems,
    )
    height = place[0]
    live = (iota((1, CELLS), 1) >> 4) < height
    masked[...] = jnp.where(live, grad[...].astype(f32), 0.0).astype(bf16)
    value = jnp.where(live, latent[...].astype(f32), 0.0)
    chan_sum = jnp.sum(value, axis=1, keepdims=True)
    chan_square = jnp.sum(value * value, axis=1, keepdims=True)
    lane = iota((CHANNELS, 128), 1)
    group = group_of((CHANNELS, 128), 0)
    terms = jnp.where(lane == group, chan_sum, 0.0)
    terms += jnp.where(lane == group + GROUPS, chan_square, 0.0)
    cells = (height * COLUMNS).astype(f32)
    stats = jnp.sum(terms, axis=0, keepdims=True)
    stats += jnp.where(iota((1, 128), 1) == 2 * GROUPS, cells, 0.0)
    row = iota((16, 128), 0)
    extra = jnp.zeros((16, 128), f32)
    for n, piece in enumerate(pieces_in(stats)):
        extra += jnp.where(row == SPARE + n, piece, 0.0)
    extra = jnp.concatenate([extra, jnp.zeros((16, 128), f32)], axis=1)
    left[...] = jnp.zeros((16, 256), f32)
    right[...] = jnp.zeros((16, 256), f32)
    left[:10, :180] = w_spatial[...].astype(f32)
    right[:10, :60] = w_temporal[...].astype(f32)
    block = (left[...] + pltpu.roll(right[...], 180, 1) + extra).astype(bf16)
    for n in range(16):
        out[n] = block


def row_move(set_index, first):
    cell = iota((CELLS, 128), 0)
    lane = iota((CELLS, 128), 1)
    inside = (lane >> 4) == set_index
    return zero_one(inside & (cell == first + (lane & 15)))


def rows_kernel(place, latent, g_next, g_here, g_last, row_first, row_last):
    last = (place[0] - 1) * COLUMNS
    head = jnp.zeros((CHANNELS, 128), f32)
    tail = jnp.zeros((CHANNELS, 128), f32)
    for n, ref in enumerate((latent, g_next, g_here, g_last)):
        head += dot(ref[...], row_move(n, 0))
        tail += dot(ref[...], row_move(n, last))
    row_first[...] = (head[:160] + pltpu.roll(head[160:], 64, 1)).astype(bf16)
    row_last[...] = (tail[:160] + pltpu.roll(tail[160:], 64, 1)).astype(bf16)


def pack_kernel(blocks, out):
    total = jnp.zeros((64, PACK), f32)
    stats = jnp.zeros((64, 128), f32)
    for z_low in range(4):
        rows = jnp.concatenate([blocks[4 * a + z_low] for a in range(4)], axis=0)
        total += dot(rows, column_place(z_low))
        stats += rows[:, :128].astype(f32)
    packed = dot(row_place((40, 64), 0, 1), total.astype(bf16))
    row = iota((64, 128), 0) & 15
    stats = jnp.where((row >= SPARE) & (row < SPARE + 3), stats, 0.0)
    stats = jnp.sum(stats, axis=0, keepdims=True)
    line = iota((40, 128), 0)
    lane = iota((40, 128), 1)
    wanted = (line, line + GROUPS, 0 * line + 2 * GROUPS)
    tile = packed[:, TILE_AT:WIDE]
    for q in range(3):
        mask = (lane == wanted[q]) & ((line < GROUPS) | (q == 2))
        column = jnp.sum(jnp.where(mask, stats, 0.0), axis=1, keepdims=True)
        for n, piece in enumerate(pieces_in(column)):
            tile += jnp.where(lane == FREE + 3 * q + n, piece, 0.0)
    packed = with_tile(packed, tile).astype(bf16)
    for n in range(16):
        out[n] = packed


def stat_columns(w_own, w_other):
    halves = []
    for ref in (w_own, w_other):
        half = jnp.zeros((40, 128), f32)
        for y in range(4):
            tile = ref[y, :, TILE_AT:WIDE].astype(f32).reshape(4, 40, 128)
            half += tile[0] + tile[1] + tile[2] + tile[3]
        halves.append(half)
    total = halves[0] + halves[1]
    line = iota((40, 128), 0)
    lane = iota((40, 128), 1)

    def quantity(q):
        mask = (lane >= FREE + 3 * q) & (lane < FREE + 3 * q + 3)
        return jnp.sum(jnp.where(mask, total, 0.0), axis=1, keepdims=True)

    def pick(q):
        across = jnp.sum(jnp.where(line == lane, quantity(q), 0.0), axis=0, keepdims=True)
        wide = iota((CHANNELS, 128), 1)
        group = group_of((CHANNELS, 128), 0)
        return jnp.sum(jnp.where(wide == group, across, 0.0), axis=1, keepdims=True)

    positions = quantity(2)[:1]
    count = positions * GROUP_SIZE
    mean = pick(0) / count
    rstd = lax.rsqrt(pick(1) / count - mean * mean + EPSILON)
    return positions, mean, rstd


def sums_split(value):
    first = rounded(value)
    return first + pltpu.roll(rounded(value - first), 16, 1)


def sums_joined(tile):
    lane = iota((40, 128), 1)
    mask = (lane >= FREE) & (lane < FREE + 16)
    return jnp.where(mask, tile + pltpu.roll(tile, 112, 1), 0.0)


def pair_kernel(own, other, out):
    lane = iota((40, 128), 1)

    def body(n, _):
        total = own[n].astype(f32) + other[n].astype(f32)
        tile = total[:, TILE_AT:WIDE]
        tile = jnp.where(lane < FREE, tile, sums_split(sums_joined(tile)))
        out[n] = with_tile(total, tile).astype(bf16)
        return 0

    lax.fori_loop(0, 16, body, 0, unroll=4)


def unpack_kernel(terms, out):
    total = terms[0].astype(f32)
    for n in range(1, 16):
        total += terms[n].astype(f32)
    sums = pltpu.roll(sums_joined(total[:, TILE_AT:WIDE]), 128 - FREE, 1)
    for step in (16, 32, 64):
        sums += pltpu.roll(sums, step, 1)
    mine = (iota((40, 128), 1) >> 4) == (iota((40, 128), 0) & 7)
    sums = jnp.sum(jnp.where(mine, sums, 0.0).reshape(5, 8, 128), axis=1)
    first = rounded(sums)
    sums = jnp.concatenate([first, rounded(sums - first)], axis=1)
    row = iota((16, 256), 0)
    extra = jnp.zeros((16, 256), f32)
    for n in range(5):
        extra += jnp.where(row == SPARE + n, sums[n : n + 1], 0.0)
    rows = dot(row_place((64, 40), 1, 0), total.astype(bf16)).astype(bf16)
    for z_low in range(4):
        block = dot_nt(rows, column_place(z_low))
        for a in range(4):
            out[4 * a + z_low] = (block[16 * a : 16 * a + 16] + extra).astype(bf16)


def turned(row):
    eye = iota((CHANNELS, CHANNELS), 0) == iota((CHANNELS, CHANNELS), 1)
    return jnp.sum(jnp.where(eye, row, 0.0), axis=1, keepdims=True)


def turned_back(column):
    eye = iota((CHANNELS, CHANNELS), 0) == iota((CHANNELS, CHANNELS), 1)
    return jnp.sum(jnp.where(eye, column, 0.0), axis=0, keepdims=True)


def pieces_of(start, stop, span):
    while start < stop:
        end = min(stop, (start // span + 1) * span)
        yield start // span, start % span, start, end - start
        start = end


def ready_kernel(
    place, order, latent, g_here, above, below, g_next, g_last, latent_ext, packed, moves
):
    height = place[0]
    to_packed = zero_one(order[...] == iota((CHANNELS, CHANNELS), 1))

    def extended(own, set_index):
        source = iota((128, 128), 0)
        lane = iota((128, 128), 1)
        rows = []
        for half in range(2):
            from_set = (source >> 4) == 4 * half + set_index
            low = from_set & (lane == (source & 15))
            high = from_set & (lane == (source & 15) + (ABOVE - BELOW))
            rows.append(dot(below[...], zero_one(low)) + dot(above[...], zero_one(high)))
        rows = jnp.concatenate(rows, axis=0)
        return jnp.concatenate([own, rows.astype(bf16)], axis=1)

    latent_ext[...] = extended(latent[...], 0)
    for k, ref in enumerate((g_next, g_here, g_last)):
        packed[k] = dot(to_packed, extended(ref[...], 1 + k)).astype(bf16)
    cell = iota((1, CELLS), 1)
    source = iota((EXT, CELLS), 0)
    for k in range(9):
        row = (cell >> 4) + (k // 3 - 1)
        column = (cell & 15) + (k % 3 - 1)
        base = jnp.where(row < 0, ABOVE, jnp.where(row == height, BELOW, row * COLUMNS))
        wanted = jnp.where((column >= 0) & (column < COLUMNS), base + column, -1)
        moves[k] = zero_one(source == wanted)


def main_kernel(
    place, gain, shift, order, order_row, latent, packed, moves, w_own, w_other,
    grad_own, grad_other, pre_grad, norm, cols, turned_s, turned_t, frames, taps,
):
    height = place[0]
    strip = place[1]

    lane = iota((1, EXT), 1)
    live = ((lane < CELLS) & ((lane >> 4) < height)) | (
        (lane >= BELOW) & (lane < BELOW + COLUMNS) & (strip < STRIPS - 1)
    ) | ((lane >= ABOVE) & (strip > 0))
    to_packed = zero_one(order[...] == iota((CHANNELS, CHANNELS), 1))
    to_plain = zero_one(iota((CHANNELS, CHANNELS), 0) == order_row[...])

    for y in range(4):
        whole = jnp.concatenate([w_own[y], w_other[y]], axis=0)
        across = whole.T
        turned_s[y * SPAN : (y + 1) * SPAN, :] = across[:SPAN]
        turned_t[y * SPAN_T : (y + 1) * SPAN_T, :] = across[WIDE : WIDE + SPAN_T]

    positions, mean, rstd = stat_columns(w_own, w_other)
    lane_n = iota((CHANNELS, 128), 1)
    norm[...] = jnp.where(lane_n == 0, mean, jnp.where(lane_n == 1, rstd, positions))
    gain_column = turned(gain[...])
    shift_column = turned(shift[...])
    normed = (latent[...].astype(f32) - mean) * rstd
    pre_act = gain_column * normed + shift_column
    sigmoid = 1.0 / (1.0 + jnp.exp(-pre_act))
    active = jnp.where(live, pre_act * sigmoid, 0.0).astype(bf16)

    grad_spat = jnp.zeros((CHANNELS, EXT), f32)
    for k in range(3):
        taps[:, k * CELLS : (k + 1) * CELLS] = packed[k, :, :CELLS]
        grad_spat += dot(turned_t[k * CHANNELS : (k + 1) * CHANNELS, :], packed[k])
    grad_spat = jnp.where(live, grad_spat, 0.0).astype(bf16)
    spat_packed = dot(to_packed, grad_spat).astype(bf16)

    for y in range(4):
        cols[y, SPAN:, :] = jnp.zeros((WIDE - SPAN, CELLS), bf16)
    grad_act = jnp.zeros((CHANNELS, CELLS), f32)
    for k in range(9):
        move = moves[k]
        moved = dot(active, move).astype(bf16)
        for y, at, start, size in pieces_of(k * CHANNELS, (k + 1) * CHANNELS, SPAN):
            first = start - k * CHANNELS
            cols[y, at : at + size, :] = moved[first : first + size]
        back = 8 - k
        grad_act += dot(
            turned_s[back * CHANNELS : (back + 1) * CHANNELS, :],
            dot(spat_packed, move).astype(bf16),
        )

    own_live = live[:, :CELLS]
    act = pre_act[:, :CELLS]
    sig = sigmoid[:, :CELLS]
    grad_pre = jnp.where(own_live, grad_act * sig * (1.0 + act * (1.0 - sig)), 0.0)
    pre_grad[...] = grad_pre
    chan_gain = jnp.sum(grad_pre * normed[:, :CELLS], axis=1, keepdims=True)
    chan_shift = jnp.sum(grad_pre, axis=1, keepdims=True)
    spot = (iota((CHANNELS, 128), 0) & 7) + FREE
    sums = jnp.where(lane_n == spot, chan_gain, 0.0)
    sums += jnp.where(lane_n == spot + 8, chan_shift, 0.0)
    sums = sums_split(jnp.sum(sums.reshape(40, 8, 128), axis=1))
    sums = jnp.concatenate([sums] * 4, axis=0)

    spatial = jnp.zeros((CHANNELS, CELLS), f32)
    left = spat_packed[:, :CELLS]
    for y in range(4):
        whole = jnp.concatenate([w_own[y, :, :WIDE], w_other[y, :, :WIDE]], axis=0)
        spatial += dot(whole, cols[y])
        part = dot_nt(left, cols[y])
        for half, ref in ((part[:160], grad_own), (part[160:], grad_other)):
            ref[y, :, :TILE_AT] = half[:, :TILE_AT].astype(bf16)
            ref[y, :, TILE_AT:WIDE] = (half[:, TILE_AT:] + sums).astype(bf16)
    spatial = jnp.where(own_live, spatial, 0.0).astype(bf16)
    spatial = dot(to_plain, spatial).astype(bf16)

    frames[...] = jnp.zeros(frames.shape, bf16)
    for k in range(3):
        for y, at, start, size in pieces_of(k * CHANNELS, (k + 1) * CHANNELS, SPAN_T):
            first = start - k * CHANNELS
            frames[y, at : at + size, k * CELLS : (k + 1) * CELLS] = spatial[first : first + size]
    for y in range(4):
        part = dot_nt(taps[...], frames[y]).astype(bf16)
        grad_own[y, :, WIDE:] = part[:160]
        grad_other[y, :, WIDE:] = part[160:]


def end_kernel(
    place, norm, gain, latent, g_here, pre_grad, terms,
    result, grad_s, grad_t, grad_gain, grad_shift,
):
    height = place[0]
    own_live = (iota((1, CELLS), 1) >> 4) < height
    mean, rstd, positions = norm[:, 0:1], norm[:, 1:2], norm[:1, 2:3]
    scale = lax.rsqrt(positions)
    count = positions * GROUP_SIZE
    total = terms[0].astype(f32)
    for n in range(1, 16):
        total += terms[n].astype(f32)
    scaled = total * scale
    grad_s[...] = scaled[:10, :180]
    grad_t[...] = pltpu.roll(scaled, 76, 1)[:10, :60]
    sums = total[:, :128] + total[:, 128:]
    wide = [jnp.broadcast_to(sums[SPARE + n : SPARE + n + 1], (64, 128)) for n in range(5)]
    wide = jnp.concatenate(wide, axis=0)
    channel = iota((CHANNELS, 128), 0)
    spot = ((channel >> 3) & 7) * 16 + (channel & 7)
    lane = iota((CHANNELS, 128), 1)
    square = (CHANNELS, CHANNELS)
    same = group_of(square, 0) == group_of(square, 1)

    def chan_row(offset):
        column = jnp.sum(jnp.where(lane == spot + offset, wide, 0.0), axis=1, keepdims=True)
        return turned_back(column)

    def over_group(row):
        return jnp.sum(jnp.where(same, gain[...] * row, 0.0), axis=1, keepdims=True) / count

    gain_row = chan_row(0)
    shift_row = chan_row(8)
    grad_gain[...] = (gain_row * scale).reshape(CHANNELS)
    grad_shift[...] = (shift_row * scale).reshape(CHANNELS)
    normed = (latent[...].astype(f32) - mean) * rstd
    value = g_here[...].astype(f32) + rstd * (
        turned(gain[...]) * pre_grad[...] - over_group(shift_row) - normed * over_group(gain_row)
    )
    result[...] = jnp.where(own_live, value, 0.0).astype(bf16)


def call(kernel, outs, smem=0, scratch=(), inputs=1, apart=0, space=pltpu.HBM, flops=0, moved=0, room=16):
    vmem = pl.BlockSpec(memory_space=pltpu.VMEM)
    specs = [pl.BlockSpec(memory_space=pltpu.SMEM)] * smem + [vmem] * (inputs - smem)
    for n in range(*apart) if apart else ():
        specs[n] = pl.BlockSpec(memory_space=space)
    many = isinstance(outs, tuple)
    return pl.pallas_call(
        kernel,
        out_shape=outs,
        in_specs=specs,
        out_specs=tuple(vmem for _ in outs) if many else vmem,
        scratch_shapes=list(scratch),
        compiler_params=pltpu.CompilerParams(vmem_limit_bytes=room << 20),
        cost_estimate=pl.CostEstimate(flops=flops, bytes_accessed=moved, transcendentals=0),
    )


def shape(dims, kind):
    return jax.ShapeDtypeStruct(dims, kind)


def step_by(value, axes, by):
    peers = lax.axis_size(axes)
    pairs = [(i, i + by) for i in range(peers) if 0 <= i + by < peers]
    return lax.ppermute(value, axes, pairs)


def swap_cores(value):
    return lax.ppermute(value, "tile_2", [(0, 1), (1, 0)])


def local(latents, out_grad, w_spatial, w_temporal, norm_gain, norm_shift, heights):
    height = heights[0]
    core = lax.axis_index("tile_2")
    place = jnp.stack([height, lax.axis_index(TILE)]).astype(jnp.int32)
    latent = latents[0]
    field = (CHANNELS, CELLS)

    near, grad = call(
        start_kernel,
        (shape((16, 16, 256), bf16), shape(field, bf16)),
        smem=1,
        inputs=5,
        apart=(1, 5),
        scratch=(
            pltpu.VMEM(field, bf16),
            pltpu.VMEM(field, bf16),
            pltpu.VMEM((10, 180), bf16),
            pltpu.VMEM((10, 60), bf16),
            pltpu.VMEM((16, 256), f32),
            pltpu.VMEM((16, 256), f32),
            pltpu.SemaphoreType.DMA((4,)),
        ),
        flops=1 << 20,
        moved=1 << 18,
        room=58,
    )(heights, latent, out_grad[0], w_spatial, w_temporal)

    grad_last = step_by(grad, FRAME, 1)
    grad_next = step_by(grad, FRAME, -1)
    near = exchange(near, ROW_Z)
    near, grad_last, grad_next = lax.optimization_barrier((near, grad_last, grad_next))
    packed = call(pack_kernel, shape((16, 40, PACK), bf16), flops=1 << 27, moved=3 << 19)(near)
    w_own = exchange(packed, PLANE).reshape(4, 160, PACK)

    row_tile = shape((CHANNELS // 2, 128), bf16)
    row_first, row_last = call(
        rows_kernel, (row_tile, row_tile), smem=1, inputs=5, flops=1 << 28, moved=1 << 20
    )(place, latent, grad_next, grad, grad_last)
    above = step_by(row_last, TILE, 1)
    below = step_by(row_first, TILE, -1)
    w_own, above, below = lax.optimization_barrier((w_own, above, below))
    w_other = swap_cores(w_own)

    packed_row = jnp.arange(CHANNELS, dtype=jnp.int32)
    half, rest = packed_row // 160, packed_row % 160
    order = rest // 40 * 80 + rest % 40 // 10 * 20 + rest % 10
    order = order + jnp.where(half == 0, core, 1 - core) * 10
    gain_row, shift_row = norm_gain[None], norm_shift[None]
    latent_ext, packed_grad, moves = call(
        ready_kernel,
        (
            shape((CHANNELS, EXT), bf16),
            shape((3, CHANNELS, EXT), bf16),
            shape((9, EXT, CELLS), bf16),
        ),
        smem=1,
        inputs=8,
        flops=1 << 29,
        moved=1 << 21,
    )(place, order[:, None], latent, grad, above, below, grad_next, grad_last)
    block = shape((4, 160, PACK), bf16)
    grad_own, grad_other, pre_grad, norm = call(
        main_kernel,
        (block, block, shape((CHANNELS, CELLS), f32), shape((CHANNELS, 128), f32)),
        smem=1,
        inputs=10,
        scratch=(
            pltpu.VMEM((4, WIDE, CELLS), bf16),
            pltpu.VMEM((4 * SPAN, CHANNELS), bf16),
            pltpu.VMEM((4 * SPAN_T, CHANNELS), bf16),
            pltpu.VMEM((4, CELLS, 3 * CELLS), bf16),
            pltpu.VMEM((CHANNELS, 3 * CELLS), bf16),
        ),
        flops=5 << 30,
        moved=8 << 20,
        room=28,
    )(
        place, gain_row, shift_row, order[:, None], order[None, :], latent_ext,
        packed_grad, moves, w_own, w_other,
    )

    blocks = (16, 40, PACK)
    pair = call(pair_kernel, shape(blocks, bf16), inputs=2, flops=1 << 20, moved=1 << 22)(
        grad_own.reshape(blocks), swap_cores(grad_other).reshape(blocks)
    )
    terms = exchange(pair, PLANE)
    parts = call(unpack_kernel, shape((16, 16, 256), bf16), flops=1 << 27, moved=1 << 21)(terms)
    parts = exchange(parts, ROW_Z)
    grad_input, grad_spatial, grad_temporal, grad_gain, grad_shift = call(
        end_kernel,
        (
            shape((CHANNELS, CELLS), bf16),
            shape((10, 180), f32),
            shape((10, 60), f32),
            shape((CHANNELS,), f32),
            shape((CHANNELS,), f32),
        ),
        smem=1,
        inputs=7,
        flops=1 << 22,
        moved=1 << 20,
    )(
        place, norm, gain_row, latent, grad, pre_grad, parts,
    )
    return grad_input[None], grad_spatial, grad_temporal, grad_gain, grad_shift


def solution(mesh):
    split = Mesh(
        mesh.devices.reshape(4, 4, 4, 4, 2), ("frame_0", "frame_1", "tile_0", "tile_1", "tile_2")
    )
    placed = (
        P(FRAME, None, TILE),
        P(FRAME, None, TILE),
        P(TILE, FRAME),
        P(TILE, FRAME),
        P(),
        P(),
        P(TILE),
    )
    return jax.shard_map(
        local,
        mesh=split,
        in_specs=placed,
        out_specs=(P(FRAME, None, TILE), P(TILE, FRAME), P(TILE, FRAME), P(), P()),
        check_vma=False,
    )
```

```python
import jax
import jax.numpy as jnp
from jax import lax
from jax.experimental import pallas as pl
from jax.experimental.pallas import tpu as pltpu
from jax.sharding import Mesh
from jax.sharding import PartitionSpec as P

GROUPS = 32
GROUP_SIZE = 10
CHANNELS = 320
COLUMNS = 16
STRIPS = 32
CELLS = 256
EXT = 384
BELOW = 256
ABOVE = 368
SPAN = 720
SPAN_T = 240
WIDE = 768
PACK = 1024
EPSILON = 1e-05
SPARE = 10
TILE_AT = 640
FREE = 80

TILE = ("tile_0", "tile_1", "tile_2")
FRAME = ("frame_0", "frame_1")
ROW_Z = ("tile_1", "frame_1")
PLANE = ("frame_0", "tile_0")

bf16 = jnp.bfloat16
f32 = jnp.float32
NT = (((1,), (1,)), ((), ()))


def iota(shape, dim):
    return lax.broadcasted_iota(jnp.int32, shape, dim)


def group_of(dims, dim):
    return (iota(dims, dim) * 6554) >> 16


def dot(a, b):
    return jnp.dot(a, b, preferred_element_type=f32)


def dot_nt(a, b):
    return lax.dot_general(a, b, NT, preferred_element_type=f32)


def zero_one(mask):
    return jnp.where(mask, 1.0, 0.0).astype(bf16)


def exchange(blocks, axes):
    return lax.all_to_all(blocks, axes, 0, 0, tiled=True)


def column_place(z_low):
    source = iota((256, PACK), 0)
    place = iota((256, PACK), 1)
    spatial = (source < 180) & (place == source + z_low * 180)
    temporal = (source >= 180) & (source < 240)
    temporal &= place == source + (WIDE - 180 + z_low * 60)
    return zero_one(spatial | temporal)


def row_place(shape, dim_small, dim_padded):
    small = iota(shape, dim_small)
    padded = iota(shape, dim_padded)
    match = small < 0
    for a in range(4):
        match |= (small >= 10 * a) & (small < 10 * a + 10) & (padded == small + 6 * a)
    return zero_one(match)


def rounded(value):
    return value.astype(bf16).astype(f32)


def pieces_in(value):
    first = rounded(value)
    second = rounded(value - first)
    return first, second, rounded(value - first - second)


def with_tile(block, tile):
    return jnp.concatenate([block[:, :TILE_AT], tile, block[:, WIDE:]], axis=1)


def fetched(pairs, sems):
    copies = [pltpu.make_async_copy(a, b, sems.at[n]) for n, (a, b) in enumerate(pairs)]
    for copy in copies:
        copy.start()
    for copy in copies:
        copy.wait()


def start_kernel(
    place, latent_at, grad_at, w_spatial_at, w_temporal_at, out, masked,
    latent, grad, w_spatial, w_temporal, left, right, sems,
):
    fetched(
        (
            (latent_at, latent),
            (grad_at, grad),
            (w_spatial_at, w_spatial),
            (w_temporal_at, w_temporal),
        ),
        sems,
    )
    height = place[0]
    live = (iota((1, CELLS), 1) >> 4) < height
    masked[...] = jnp.where(live, grad[...].astype(f32), 0.0).astype(bf16)
    value = jnp.where(live, latent[...].astype(f32), 0.0)
    chan_sum = jnp.sum(value, axis=1, keepdims=True)
    chan_square = jnp.sum(value * value, axis=1, keepdims=True)
    lane = iota((CHANNELS, 128), 1)
    group = group_of((CHANNELS, 128), 0)
    terms = jnp.where(lane == group, chan_sum, 0.0)
    terms += jnp.where(lane == group + GROUPS, chan_square, 0.0)
    cells = (height * COLUMNS).astype(f32)
    stats = jnp.sum(terms, axis=0, keepdims=True)
    stats += jnp.where(iota((1, 128), 1) == 2 * GROUPS, cells, 0.0)
    row = iota((16, 128), 0)
    extra = jnp.zeros((16, 128), f32)
    for n, piece in enumerate(pieces_in(stats)):
        extra += jnp.where(row == SPARE + n, piece, 0.0)
    extra = jnp.concatenate([extra, jnp.zeros((16, 128), f32)], axis=1)
    left[...] = jnp.zeros((16, 256), f32)
    right[...] = jnp.zeros((16, 256), f32)
    left[:10, :180] = w_spatial[...].astype(f32)
    right[:10, :60] = w_temporal[...].astype(f32)
    block = (left[...] + pltpu.roll(right[...], 180, 1) + extra).astype(bf16)
    for n in range(16):
        out[n] = block


def row_move(set_index, first):
    cell = iota((CELLS, 128), 0)
    lane = iota((CELLS, 128), 1)
    inside = (lane >> 4) == set_index
    return zero_one(inside & (cell == first + (lane & 15)))


def rows_kernel(place, latent, g_next, g_here, g_last, row_first, row_last):
    last = (place[0] - 1) * COLUMNS
    head = jnp.zeros((CHANNELS, 128), f32)
    tail = jnp.zeros((CHANNELS, 128), f32)
    for n, ref in enumerate((latent, g_next, g_here, g_last)):
        head += dot(ref[...], row_move(n, 0))
        tail += dot(ref[...], row_move(n, last))
    row_first[...] = (head[:160] + pltpu.roll(head[160:], 64, 1)).astype(bf16)
    row_last[...] = (tail[:160] + pltpu.roll(tail[160:], 64, 1)).astype(bf16)


def pack_kernel(blocks, out):
    total = jnp.zeros((64, PACK), f32)
    stats = jnp.zeros((64, 128), f32)
    for z_low in range(4):
        rows = jnp.concatenate([blocks[4 * a + z_low] for a in range(4)], axis=0)
        total += dot(rows, column_place(z_low))
        stats += rows[:, :128].astype(f32)
    packed = dot(row_place((40, 64), 0, 1), total.astype(bf16))
    row = iota((64, 128), 0) & 15
    stats = jnp.where((row >= SPARE) & (row < SPARE + 3), stats, 0.0)
    stats = jnp.sum(stats, axis=0, keepdims=True)
    line = iota((40, 128), 0)
    lane = iota((40, 128), 1)
    wanted = (line, line + GROUPS, 0 * line + 2 * GROUPS)
    tile = packed[:, TILE_AT:WIDE]
    for q in range(3):
        mask = (lane == wanted[q]) & ((line < GROUPS) | (q == 2))
        column = jnp.sum(jnp.where(mask, stats, 0.0), axis=1, keepdims=True)
        for n, piece in enumerate(pieces_in(column)):
            tile += jnp.where(lane == FREE + 3 * q + n, piece, 0.0)
    packed = with_tile(packed, tile).astype(bf16)
    for n in range(16):
        out[n] = packed


def stat_columns(w_own, w_other):
    halves = []
    for ref in (w_own, w_other):
        half = jnp.zeros((40, 128), f32)
        for y in range(4):
            tile = ref[y, :, TILE_AT:WIDE].astype(f32).reshape(4, 40, 128)
            half += tile[0] + tile[1] + tile[2] + tile[3]
        halves.append(half)
    total = halves[0] + halves[1]
    line = iota((40, 128), 0)
    lane = iota((40, 128), 1)

    def quantity(q):
        mask = (lane >= FREE + 3 * q) & (lane < FREE + 3 * q + 3)
        return jnp.sum(jnp.where(mask, total, 0.0), axis=1, keepdims=True)

    def pick(q):
        across = jnp.sum(jnp.where(line == lane, quantity(q), 0.0), axis=0, keepdims=True)
        wide = iota((CHANNELS, 128), 1)
        group = group_of((CHANNELS, 128), 0)
        return jnp.sum(jnp.where(wide == group, across, 0.0), axis=1, keepdims=True)

    positions = quantity(2)[:1]
    count = positions * GROUP_SIZE
    mean = pick(0) / count
    rstd = lax.rsqrt(pick(1) / count - mean * mean + EPSILON)
    return positions, mean, rstd


def sums_split(value):
    first = rounded(value)
    return first + pltpu.roll(rounded(value - first), 16, 1)


def sums_joined(tile):
    lane = iota((40, 128), 1)
    mask = (lane >= FREE) & (lane < FREE + 16)
    return jnp.where(mask, tile + pltpu.roll(tile, 112, 1), 0.0)


def pair_kernel(own, other, out):
    lane = iota((40, 128), 1)

    def body(n, _):
        total = own[n].astype(f32) + other[n].astype(f32)
        tile = total[:, TILE_AT:WIDE]
        tile = jnp.where(lane < FREE, tile, sums_split(sums_joined(tile)))
        out[n] = with_tile(total, tile).astype(bf16)
        return 0

    lax.fori_loop(0, 16, body, 0, unroll=4)


def unpack_kernel(terms, out):
    total = terms[0].astype(f32)
    for n in range(1, 16):
        total += terms[n].astype(f32)
    sums = pltpu.roll(sums_joined(total[:, TILE_AT:WIDE]), 128 - FREE, 1)
    for step in (16, 32, 64):
        sums += pltpu.roll(sums, step, 1)
    mine = (iota((40, 128), 1) >> 4) == (iota((40, 128), 0) & 7)
    sums = jnp.sum(jnp.where(mine, sums, 0.0).reshape(5, 8, 128), axis=1)
    first = rounded(sums)
    sums = jnp.concatenate([first, rounded(sums - first)], axis=1)
    row = iota((16, 256), 0)
    extra = jnp.zeros((16, 256), f32)
    for n in range(5):
        extra += jnp.where(row == SPARE + n, sums[n : n + 1], 0.0)
    rows = dot(row_place((64, 40), 1, 0), total.astype(bf16)).astype(bf16)
    for z_low in range(4):
        block = dot_nt(rows, column_place(z_low))
        for a in range(4):
            out[4 * a + z_low] = (block[16 * a : 16 * a + 16] + extra).astype(bf16)


def turned(row):
    eye = iota((CHANNELS, CHANNELS), 0) == iota((CHANNELS, CHANNELS), 1)
    return jnp.sum(jnp.where(eye, row, 0.0), axis=1, keepdims=True)


def turned_back(column):
    eye = iota((CHANNELS, CHANNELS), 0) == iota((CHANNELS, CHANNELS), 1)
    return jnp.sum(jnp.where(eye, column, 0.0), axis=0, keepdims=True)


def pieces_of(start, stop, span):
    while start < stop:
        end = min(stop, (start // span + 1) * span)
        yield start // span, start % span, start, end - start
        start = end


def ready_kernel(
    place, order, latent, g_here, above, below, g_next, g_last, latent_ext, packed, moves
):
    height = place[0]
    to_packed = zero_one(order[...] == iota((CHANNELS, CHANNELS), 1))

    def extended(own, set_index):
        source = iota((128, 128), 0)
        lane = iota((128, 128), 1)
        rows = []
        for half in range(2):
            from_set = (source >> 4) == 4 * half + set_index
            low = from_set & (lane == (source & 15))
            high = from_set & (lane == (source & 15) + (ABOVE - BELOW))
            rows.append(dot(below[...], zero_one(low)) + dot(above[...], zero_one(high)))
        rows = jnp.concatenate(rows, axis=0)
        return jnp.concatenate([own, rows.astype(bf16)], axis=1)

    latent_ext[...] = extended(latent[...], 0)
    for k, ref in enumerate((g_next, g_here, g_last)):
        packed[k] = dot(to_packed, extended(ref[...], 1 + k)).astype(bf16)
    cell = iota((1, CELLS), 1)
    source = iota((EXT, CELLS), 0)
    for k in range(9):
        row = (cell >> 4) + (k // 3 - 1)
        column = (cell & 15) + (k % 3 - 1)
        base = jnp.where(row < 0, ABOVE, jnp.where(row == height, BELOW, row * COLUMNS))
        wanted = jnp.where((column >= 0) & (column < COLUMNS), base + column, -1)
        moves[k] = zero_one(source == wanted)


def main_kernel(
    place, gain, shift, order, order_row, latent, packed, moves, w_own, w_other,
    grad_other, pre_grad, norm, cols, frames, taps, left, tile_sums, turned_s, turned_t,
):
    height = place[0]
    strip = place[1]

    lane = iota((1, EXT), 1)
    live = ((lane < CELLS) & ((lane >> 4) < height)) | (
        (lane >= BELOW) & (lane < BELOW + COLUMNS) & (strip < STRIPS - 1)
    ) | ((lane >= ABOVE) & (strip > 0))
    to_packed = zero_one(order[...] == iota((CHANNELS, CHANNELS), 1))
    to_plain = zero_one(iota((CHANNELS, CHANNELS), 0) == order_row[...])

    for y in range(4):
        whole = jnp.concatenate([w_own[y], w_other[y]], axis=0)
        across = whole.T
        turned_s[y * SPAN : (y + 1) * SPAN, :] = across[:SPAN]
        turned_t[y * SPAN_T : (y + 1) * SPAN_T, :] = across[WIDE : WIDE + SPAN_T]

    positions, mean, rstd = stat_columns(w_own, w_other)
    lane_n = iota((CHANNELS, 128), 1)
    norm[...] = jnp.where(lane_n == 0, mean, jnp.where(lane_n == 1, rstd, positions))
    gain_column = turned(gain[...])
    shift_column = turned(shift[...])
    normed = (latent[...].astype(f32) - mean) * rstd
    pre_act = gain_column * normed + shift_column
    sigmoid = 1.0 / (1.0 + jnp.exp(-pre_act))
    active = jnp.where(live, pre_act * sigmoid, 0.0).astype(bf16)

    grad_spat = jnp.zeros((CHANNELS, EXT), f32)
    for k in range(3):
        grad_spat += dot(turned_t[k * CHANNELS : (k + 1) * CHANNELS, :], packed[k])
    packed_taps = jnp.concatenate([packed[k, :, :CELLS] for k in range(3)], axis=1)
    grad_spat = jnp.where(live, grad_spat, 0.0).astype(bf16)
    spat_packed = dot(to_packed, grad_spat).astype(bf16)

    for y in range(4):
        cols[y, SPAN:, :] = jnp.zeros((WIDE - SPAN, CELLS), bf16)
    grad_act = jnp.zeros((CHANNELS, CELLS), f32)
    for k in range(9):
        move = moves[k]
        moved = dot(active, move).astype(bf16)
        for y, at, start, size in pieces_of(k * CHANNELS, (k + 1) * CHANNELS, SPAN):
            first = start - k * CHANNELS
            cols[y, at : at + size, :] = moved[first : first + size]
        back = 8 - k
        grad_act += dot(
            turned_s[back * CHANNELS : (back + 1) * CHANNELS, :],
            dot(spat_packed, move).astype(bf16),
        )

    own_live = live[:, :CELLS]
    act = pre_act[:, :CELLS]
    sig = sigmoid[:, :CELLS]
    grad_pre = jnp.where(own_live, grad_act * sig * (1.0 + act * (1.0 - sig)), 0.0)
    pre_grad[...] = grad_pre
    chan_gain = jnp.sum(grad_pre * normed[:, :CELLS], axis=1, keepdims=True)
    chan_shift = jnp.sum(grad_pre, axis=1, keepdims=True)
    spot = (iota((CHANNELS, 128), 0) & 7) + FREE
    sums = jnp.where(lane_n == spot, chan_gain, 0.0)
    sums += jnp.where(lane_n == spot + 8, chan_shift, 0.0)
    sums = sums_split(jnp.sum(sums.reshape(40, 8, 128), axis=1))
    sums = jnp.concatenate([sums] * 4, axis=0)

    tile_sums[...] = sums

    spatial = jnp.zeros((CHANNELS, CELLS), f32)
    left[...] = spat_packed[:160, :CELLS]
    for y in range(4):
        whole = jnp.concatenate([w_own[y, :, :WIDE], w_other[y, :, :WIDE]], axis=0)
        spatial += dot(whole, cols[y])
    spatial = jnp.where(own_live, spatial, 0.0).astype(bf16)
    spatial = dot(to_plain, spatial).astype(bf16)

    frames[...] = jnp.zeros(frames.shape, bf16)
    for k in range(3):
        for y, at, start, size in pieces_of(k * CHANNELS, (k + 1) * CHANNELS, SPAN_T):
            first = start - k * CHANNELS
            frames[y, at : at + size, k * CELLS : (k + 1) * CELLS] = spatial[first : first + size]
    half_gradient(grad_other, spat_packed[160:, :CELLS], packed_taps[160:], cols, frames, sums)
    taps[...] = packed_taps[:160]


def half_gradient(out, left, taps, cols, frames, sums):
    for y in range(4):
        part = dot_nt(left, cols[y])
        out[y, :, :TILE_AT] = part[:, :TILE_AT].astype(bf16)
        out[y, :, TILE_AT:WIDE] = (part[:, TILE_AT:] + sums).astype(bf16)
        out[y, :, WIDE:] = dot_nt(taps, frames[y]).astype(bf16)


def own_kernel(left, taps, cols, frames, sums, out):
    half_gradient(out, left[...], taps[...], cols, frames, sums[...])


def end_kernel(
    place, norm, gain, latent, g_here, pre_grad, terms,
    result, grad_s, grad_t, grad_gain, grad_shift,
):
    height = place[0]
    own_live = (iota((1, CELLS), 1) >> 4) < height
    mean, rstd, positions = norm[:, 0:1], norm[:, 1:2], norm[:1, 2:3]
    scale = lax.rsqrt(positions)
    count = positions * GROUP_SIZE
    total = terms[0].astype(f32)
    for n in range(1, 16):
        total += terms[n].astype(f32)
    scaled = total * scale
    grad_s[...] = scaled[:10, :180]
    grad_t[...] = pltpu.roll(scaled, 76, 1)[:10, :60]
    sums = total[:, :128] + total[:, 128:]
    wide = [jnp.broadcast_to(sums[SPARE + n : SPARE + n + 1], (64, 128)) for n in range(5)]
    wide = jnp.concatenate(wide, axis=0)
    channel = iota((CHANNELS, 128), 0)
    spot = ((channel >> 3) & 7) * 16 + (channel & 7)
    lane = iota((CHANNELS, 128), 1)
    square = (CHANNELS, CHANNELS)
    same = group_of(square, 0) == group_of(square, 1)

    def chan_row(offset):
        column = jnp.sum(jnp.where(lane == spot + offset, wide, 0.0), axis=1, keepdims=True)
        return turned_back(column)

    def over_group(row):
        return jnp.sum(jnp.where(same, gain[...] * row, 0.0), axis=1, keepdims=True) / count

    gain_row = chan_row(0)
    shift_row = chan_row(8)
    grad_gain[...] = (gain_row * scale).reshape(CHANNELS)
    grad_shift[...] = (shift_row * scale).reshape(CHANNELS)
    normed = (latent[...].astype(f32) - mean) * rstd
    value = g_here[...].astype(f32) + rstd * (
        turned(gain[...]) * pre_grad[...] - over_group(shift_row) - normed * over_group(gain_row)
    )
    result[...] = jnp.where(own_live, value, 0.0).astype(bf16)


def call(kernel, outs, smem=0, scratch=(), inputs=1, apart=0, space=pltpu.HBM, flops=0, moved=0, room=16):
    vmem = pl.BlockSpec(memory_space=pltpu.VMEM)
    specs = [pl.BlockSpec(memory_space=pltpu.SMEM)] * smem + [vmem] * (inputs - smem)
    for n in range(*apart) if apart else ():
        specs[n] = pl.BlockSpec(memory_space=space)
    many = isinstance(outs, tuple)
    return pl.pallas_call(
        kernel,
        out_shape=outs,
        in_specs=specs,
        out_specs=tuple(vmem for _ in outs) if many else vmem,
        scratch_shapes=list(scratch),
        compiler_params=pltpu.CompilerParams(vmem_limit_bytes=room << 20),
        cost_estimate=pl.CostEstimate(flops=flops, bytes_accessed=moved, transcendentals=0),
    )


def shape(dims, kind):
    return jax.ShapeDtypeStruct(dims, kind)


def step_by(value, axes, by):
    peers = lax.axis_size(axes)
    pairs = [(i, i + by) for i in range(peers) if 0 <= i + by < peers]
    return lax.ppermute(value, axes, pairs)


def swap_cores(value):
    return lax.ppermute(value, "tile_2", [(0, 1), (1, 0)])


def local(latents, out_grad, w_spatial, w_temporal, norm_gain, norm_shift, heights):
    height = heights[0]
    core = lax.axis_index("tile_2")
    place = jnp.stack([height, lax.axis_index(TILE)]).astype(jnp.int32)
    latent = latents[0]
    field = (CHANNELS, CELLS)

    near, grad = call(
        start_kernel,
        (shape((16, 16, 256), bf16), shape(field, bf16)),
        smem=1,
        inputs=5,
        apart=(1, 5),
        scratch=(
            pltpu.VMEM(field, bf16),
            pltpu.VMEM(field, bf16),
            pltpu.VMEM((10, 180), bf16),
            pltpu.VMEM((10, 60), bf16),
            pltpu.VMEM((16, 256), f32),
            pltpu.VMEM((16, 256), f32),
            pltpu.SemaphoreType.DMA((4,)),
        ),
        flops=1 << 20,
        moved=1 << 18,
        room=58,
    )(heights, latent, out_grad[0], w_spatial, w_temporal)

    packed_row = jnp.arange(CHANNELS, dtype=jnp.int32)
    half, rest = packed_row // 160, packed_row % 160
    order = rest // 40 * 80 + rest % 40 // 10 * 20 + rest % 10
    order = order + jnp.where(half == 0, core, 1 - core) * 10
    grad_last = step_by(grad, FRAME, 1)
    grad_next = step_by(grad, FRAME, -1)
    near = exchange(near, ROW_Z)
    near, order = lax.optimization_barrier((near, order))
    packed = call(pack_kernel, shape((16, 40, PACK), bf16), flops=1 << 27, moved=3 << 19)(near)
    w_own = exchange(packed, PLANE).reshape(4, 160, PACK)

    row_tile = shape((CHANNELS // 2, 128), bf16)
    row_first, row_last = call(
        rows_kernel, (row_tile, row_tile), smem=1, inputs=5, flops=1 << 28, moved=1 << 20
    )(place, latent, grad_next, grad, grad_last)
    above = step_by(row_last, TILE, 1)
    below = step_by(row_first, TILE, -1)
    w_own, above, below = lax.optimization_barrier((w_own, above, below))
    w_other = swap_cores(w_own)

    gain_row, shift_row = norm_gain[None], norm_shift[None]
    latent_ext, packed_grad, moves = call(
        ready_kernel,
        (
            shape((CHANNELS, EXT), bf16),
            shape((3, CHANNELS, EXT), bf16),
            shape((9, EXT, CELLS), bf16),
        ),
        smem=1,
        inputs=8,
        flops=1 << 29,
        moved=1 << 21,
    )(place, order[:, None], latent, grad, above, below, grad_next, grad_last)
    block = shape((4, 160, PACK), bf16)
    grad_other, pre_grad, norm, cols, frames, taps, left, tile_sums = call(
        main_kernel,
        (
            block,
            shape((CHANNELS, CELLS), f32),
            shape((CHANNELS, 128), f32),
            shape((4, WIDE, CELLS), bf16),
            shape((4, CELLS, 3 * CELLS), bf16),
            shape((160, 3 * CELLS), bf16),
            shape((160, CELLS), bf16),
            shape((160, 128), f32),
        ),
        smem=1,
        inputs=10,
        scratch=(
            pltpu.VMEM((4 * SPAN, CHANNELS), bf16),
            pltpu.VMEM((4 * SPAN_T, CHANNELS), bf16),
        ),
        flops=5 << 30,
        moved=8 << 20,
        room=28,
    )(
        place, gain_row, shift_row, order[:, None], order[None, :], latent_ext,
        packed_grad, moves, w_own, w_other,
    )

    received = swap_cores(grad_other)
    grad_own = call(own_kernel, block, inputs=5, flops=1 << 30, moved=1 << 22)(
        left, taps, cols, frames, tile_sums
    )

    blocks = (16, 40, PACK)
    pair = call(pair_kernel, shape(blocks, bf16), inputs=2, flops=1 << 20, moved=1 << 22)(
        grad_own.reshape(blocks), received.reshape(blocks)
    )
    terms = exchange(pair, PLANE)
    parts = call(unpack_kernel, shape((16, 16, 256), bf16), flops=1 << 27, moved=1 << 21)(terms)
    parts = exchange(parts, ROW_Z)
    grad_input, grad_spatial, grad_temporal, grad_gain, grad_shift = call(
        end_kernel,
        (
            shape((CHANNELS, CELLS), bf16),
            shape((10, 180), f32),
            shape((10, 60), f32),
            shape((CHANNELS,), f32),
            shape((CHANNELS,), f32),
        ),
        smem=1,
        inputs=7,
        flops=1 << 22,
        moved=1 << 20,
    )(
        place, norm, gain_row, latent, grad, pre_grad, parts,
    )
    return grad_input[None], grad_spatial, grad_temporal, grad_gain, grad_shift


def solution(mesh):
    split = Mesh(
        mesh.devices.reshape(4, 4, 4, 4, 2), ("frame_0", "frame_1", "tile_0", "tile_1", "tile_2")
    )
    placed = (
        P(FRAME, None, TILE),
        P(FRAME, None, TILE),
        P(TILE, FRAME),
        P(TILE, FRAME),
        P(),
        P(),
        P(TILE),
    )
    return jax.shard_map(
        local,
        mesh=split,
        in_specs=placed,
        out_specs=(P(FRAME, None, TILE), P(TILE, FRAME), P(TILE, FRAME), P(), P()),
        check_vma=False,
    )
```
